512 devices in a mesh: ka: 8 (over y_hi, core), pb: 16 (over y_lo, z), row: 4 (over x).
Axes of the slice: x: 4, y: 8 (y_hi: 4, y_lo: 2; y = y_hi * 2 + y_lo), z: 8, core: 2. Of those that a mesh axis runs over, the one named last changes fastest.
Arguments:
- coupling: bfloat16 [64, 64, 20736], P('pb', ('ka', 'row')), may hold values from -1 to 1
- rotation: bfloat16 [64, 36, 36], P('pb'), may hold values from -1 to 1
- freq: float32 [64, 36], P('pb'), may hold values from 0.02 to 0.3
- eigvec: bfloat16 [1024, 24, 24], P(('ka', 'row')), may hold values from -1.25 to 1.25
- energies: float32 [1024, 24], P(('ka', 'row')), may hold values from -1.5 to 1.5
- window: int32 [1024], P(('ka', 'row')), may hold values from 12 to 24
- kq_index: int32 [64, 1024], P('pb'), may hold values from 0 to 1023, as said below
- kpoints: float32 [1024, 3], replicated, may hold values from 0 to 1
- lattice: int32 [64, 3], replicated, may hold values from -3 to 3
Outputs:
- electron: float32 [1024, 24], P(('ka', 'row'))
- phonon: float32 [64, 36], P('pb')
The draws below stay inside these ranges and needn't reach their ends.
Inputs may be any that keep to these rules, and one draw needn't show every extreme that they name: The k-points form a shifted grid of 1024 points, (1024 // 64) x 8 x 8, listed in an order drawn from the seed; each q-point is a vector of that grid without the shift. kq_index[q, k] is the index of the k-point equal to kpoints[k] plus the q-point's vector modulo 1, so each row of kq_index is a permutation of 0 to 1023.
All inputs are finite; a program needn't handle non-finite values.
Results may differ from the reference program's by a relative error of at most 0.00089.
Values may be sent and summed in bfloat16 or wider, within the bound.
A program may use at most 128 MiB of HBM per device.

```python
import math
import jax
import jax.numpy as jnp
from jax import lax

NB = 24
NM = 36
NRE = 64
NK = 1024
NQ = 64


def grid_parts(grid_index):
    first = grid_index // 64
    second = grid_index // 8 % 8
    third = grid_index % 8
    return (first, second, third)


def grid_common(key):
    order = jax.random.permutation(jax.random.fold_in(key, 311), NK).astype(jnp.int32)
    q_grid = jax.random.randint(jax.random.fold_in(key, 312), (NQ,), 0, NK).astype(jnp.int32)
    start_displacement = jax.random.uniform(jax.random.fold_in(key, 313), (3,), jnp.float32)
    return (order, q_grid, start_displacement)


def draw_kpoints(key, part):
    order, q_grid, start_displacement = grid_common(key)
    first_length = NK // 64
    first, second, third = grid_parts(order)
    coords = jnp.stack([(first.astype(jnp.float32) + start_displacement[0]) / first_length, (second.astype(jnp.float32) + start_displacement[1]) / 8.0, (third.astype(jnp.float32) + start_displacement[2]) / 8.0], axis=1)
    return jnp.clip(coords, 0.0, 0.999999).astype(jnp.float32)


def draw_kq_index(key, part):
    order, q_grid, start_displacement = grid_common(key)
    first_length = NK // 64
    inverse = jnp.argsort(order).astype(jnp.int32)
    k_first, k_second, k_third = grid_parts(order)
    q_first, q_second, q_third = grid_parts(q_grid)
    s_first = (k_first[None, :] + q_first[:, None]) % first_length
    middle_offset_index = (k_second[None, :] + q_second[:, None]) % 8
    s_third = (k_third[None, :] + q_third[:, None]) % 8
    target = (s_first * 64 + middle_offset_index * 8 + s_third).astype(jnp.int32)
    return jnp.take(inverse, target, axis=0).astype(jnp.int32)


def place_ends(entries, rng, least, top_value):
    longest = entries.shape.index(max(entries.shape))
    spots = []
    for shift in (0, 1):
        where = [jax.random.randint(jax.random.fold_in(rng, axis), (), 0, length) for axis, length in enumerate(entries.shape)]
        where[longest] = (where[longest] + shift) % entries.shape[longest]
        spots.append(tuple(where))
    return entries.at[spots[0]].set(least).at[spots[1]].set(top_value)


def block_scale(rng, extent, split, least, high):
    gain, own = 1.0, jax.random.fold_in(rng, 6)
    for axis_at, shards_of in split:
        steps = jnp.exp(jax.random.uniform(jax.random.fold_in(own, axis_at), (shards_of,), jnp.float32, least / len(split), high / len(split)))
        gain = gain * jnp.repeat(steps, extent[axis_at] // shards_of).reshape([-1 if axis == axis_at else 1 for axis in range(len(extent))])
    return gain


def normal_values(key, shape, width, bound, cuts=(), held_as=jnp.bfloat16):
    values = width * jax.random.normal(key, shape, jnp.float32)
    if cuts:
        values = values * block_scale(key, shape, cuts, -0.22, 0.18)
    return jnp.clip(values, -bound, bound).astype(held_as)


def setup_inputs(seed: int = 0) -> dict:
    key_list = jax.random.split(jax.random.key(seed), 10)
    coupling = normal_values(key_list[0], (NQ, NRE, NM * NB * NB), (NRE // 2) ** -0.5, 1.0, ((0, 16), (1, 32)))
    rotation = normal_values(key_list[1], (NQ, NM, NM), NM ** -0.5, 1.0, ((0, 16),))
    freq = jnp.clip(jnp.exp(math.log(0.3) - 2.7080503 * jax.random.uniform(key_list[2], (NQ, NM), jnp.float32) ** block_scale(key_list[2], (NQ, NM), ((0, 16),), -0.2, 0.2)), 0.02, 0.3)
    eigvec = normal_values(key_list[3], (NK, NB, NB), NB ** -0.5, 1.25, ((0, 32),))
    energies = jnp.clip(jax.random.uniform(key_list[4], (NK, NB), jnp.float32, -1.5, 1.5) * block_scale(key_list[4], (NK, NB), ((0, 32),), -0.4, 0.0), -1.5, 1.5)
    window = place_ends(jax.random.randint(key_list[5], (NK,), NB // 2, NB + 1), jax.random.fold_in(key_list[5], 1), NB // 2, NB).astype(jnp.int32)
    kq_index = draw_kq_index(jax.random.fold_in(key_list[9], 71), 0)
    kpoints = draw_kpoints(jax.random.fold_in(key_list[9], 71), 0)
    lattice = place_ends(jax.random.randint(key_list[8], (NRE, 3), -3, 4), jax.random.fold_in(key_list[8], 1), -3, 3).astype(jnp.int32)
    return {"coupling": coupling, "rotation": rotation, "freq": freq, "eigvec": eigvec, "energies": energies, "window": window, "kq_index": kq_index, "kpoints": kpoints, "lattice": lattice}


SIGMA = 0.1
THERMAL_ENERGY_KT = 0.2

def phase_table(lattice, kpoint_rows):
    rvec = lattice.astype(jnp.float32)
    argument = rvec[:, 0:1] * kpoint_rows[:, 0][None, :] + rvec[:, 1:2] * kpoint_rows[:, 1][None, :] + rvec[:, 2:3] * kpoint_rows[:, 2][None, :]
    return jnp.cos(2.0 * math.pi * argument).astype(jnp.bfloat16)

def reference(coupling, rotation, freq, eigvec, energies, window, kq_index, kpoints, lattice):
    block = min(NK, 128)
    count = NK // block
    limits = window.astype(jnp.float32)
    norm = 1.0 / (math.sqrt(2.0 * math.pi) * SIGMA)
    bands = jnp.arange(NB).astype(jnp.float32)

    def per_q(items):
        coup_q, rot_q, freq_q, kq_row = items

        def per_block(number):
            start = (number * block).astype(jnp.int32)
            kp_rows = lax.dynamic_slice(kpoints, (start, jnp.int32(0)), (block, 3))
            phase = phase_table(lattice, kp_rows)
            index = lax.dynamic_slice(kq_row, (start,), (block,))
            eig_k = lax.dynamic_slice(eigvec, (start, jnp.int32(0), jnp.int32(0)), (block, NB, NB))
            eig_kq = jnp.take(eigvec, index, axis=0)
            energy_initial_state = lax.dynamic_slice(energies, (start, jnp.int32(0)), (block, NB))
            energy_final_state = jnp.take(energies, index, axis=0)
            lim_k = lax.dynamic_slice(limits, (start,), (block,))
            lim_kq = jnp.take(limits, index, axis=0)
            bloch = jnp.dot(phase.T, coup_q, preferred_element_type=jnp.float32).astype(jnp.bfloat16)
            bloch = bloch.reshape(block, NM, NB, NB)
            modal = jnp.einsum('kamn,ab->kbmn', bloch.astype(jnp.float32), rot_q.astype(jnp.float32)).astype(jnp.bfloat16)
            right = jnp.einsum('kbmj,kjn->kbmn', modal.astype(jnp.float32), eig_k.astype(jnp.float32)).astype(jnp.bfloat16)
            coupled = jnp.einsum('kim,kbin->kbmn', eig_kq.astype(jnp.float32), right.astype(jnp.float32))
            diff = energy_final_state[:, None, :, None] - energy_initial_state[:, None, None, :] - freq_q[None, :, None, None]
            delta = jnp.exp(-(diff * diff) / (2.0 * SIGMA * SIGMA)) * norm
            mask_m = (bands[None, :] < lim_kq[:, None]).astype(jnp.float32)
            mask_n = (bands[None, :] < lim_k[:, None]).astype(jnp.float32)
            strength = coupled * coupled * delta * mask_m[:, None, :, None] * mask_n[:, None, None, :]
            fermi_filling_initial = jax.nn.sigmoid(-energy_initial_state / THERMAL_ENERGY_KT)
            fermi_filling_final = jax.nn.sigmoid(-energy_final_state / THERMAL_ENERGY_KT)
            elec = lax.optimization_barrier(jnp.sum(strength, axis=(1, 2)))
            phon = lax.optimization_barrier(jnp.sum(strength * (fermi_filling_initial[:, None, None, :] - fermi_filling_final[:, None, :, None]), axis=(0, 2, 3)))
            return (elec, phon)
        elec_blocks, vibration_mode_tiles = lax.map(per_block, jnp.arange(count))
        return (elec_blocks.reshape(NK, NB), lax.optimization_barrier(jnp.sum(vibration_mode_tiles, axis=0)))
    elec_q, phon_q = lax.map(per_q, (coupling, rotation, freq, kq_index))
    electron = lax.optimization_barrier(jnp.sum(elec_q, axis=0)) * (1.0 / (NQ * NM * NB))
    phonon = phon_q * (1.0 / (NK * NB))
    return (electron, phonon)
```

```python
import math

import jax
import jax.numpy as jnp
from jax import lax
from jax.sharding import PartitionSpec as P
from jax.experimental import pallas as pl
from jax.experimental.pallas import tpu as pltpu

SIGMA = 0.1
KT = 0.2
NB, NM, NR = 24, 36, 64
NV = 9
PITCH = 32
BLOCK = 32
TILES = 8
VSLOT = [(v // 5, v % 5) for v in range(NV)]


def compute_kernel(core_ref, kq_ref, freq_ref, phase_ref, rt_ref, eig_ref, etab_ref, el_ref,
                   tab, etile, pscr, etscr, ektscr, wscr, xscr, bd, ybuf, aescr, phacc):
    f32, bf16 = jnp.float32, jnp.bfloat16
    core = core_ref[0]
    lane = lax.broadcasted_iota(jnp.int32, (1, 128), 1)
    slot_lane = lane % PITCH

    row = lax.broadcasted_iota(jnp.int32, (128, 128), 0)
    col = lax.broadcasted_iota(jnp.int32, (128, 128), 1)
    pick = jnp.where((row % PITCH == NB) & (row // PITCH == col // PITCH), 1.0, 0.0).astype(bf16)
    lim = jnp.dot(etab_ref[...].astype(bf16), pick, preferred_element_type=f32)
    etile[...] = jnp.where(slot_lane.astype(f32) < lim, 1.0, 0.0)

    def build_table(t, _):
        m = etile[pl.ds((t % 32) * TILES + t // 32, 1), :]
        tab[t] = eig_ref[t].astype(f32) * m
        return 0
    lax.fori_loop(0, 256, build_table, 0, unroll=8)

    r1 = lax.broadcasted_iota(jnp.int32, (NB, 384), 0)
    c1 = lax.broadcasted_iota(jnp.int32, (NB, 384), 1)
    spread = jnp.where(c1 % NB == r1, 1.0, 0.0).astype(bf16)
    r2 = lax.broadcasted_iota(jnp.int32, (NR, NR * NB), 0)
    c2 = lax.broadcasted_iota(jnp.int32, (NR, NR * NB), 1)
    widen = jnp.where(c2 // NB == r2, 1.0, 0.0).astype(bf16)
    r3 = lax.broadcasted_iota(jnp.int32, (256, 128), 0)
    c3 = lax.broadcasted_iota(jnp.int32, (256, 128), 1)
    fold = jnp.where(r3 // PITCH == c3, 1.0, 0.0).astype(f32)

    pscr[...] = jnp.dot(phase_ref[...], widen, preferred_element_type=f32)
    for ch in range(16):
        blk = core * 16 + ch
        ektscr[ch] = jnp.transpose(etab_ref[pl.ds(pl.multiple_of(blk * TILES, 8), TILES), :])
    bd[...] = jnp.zeros_like(bd)
    phacc[...] = jnp.zeros_like(phacc)

    def chunk(ch, _):
        blk = core * 16 + ch
        tt = jnp.concatenate([tab[32 * t + blk] for t in range(TILES)], axis=1).astype(bf16)
        etscr[...] = lax.dot_general(tt, spread, (((0,), (0,)), ((), ())), preferred_element_type=f32)

        def wtile(t, _):
            for pair in range(2):
                parts = []
                for kk in range(2):
                    k = 2 * pair + kk
                    ek = etscr[pl.ds(pl.multiple_of(t * 128 + PITCH * k, 8), NB), :]
                    p = pscr[pl.ds(ch * BLOCK + t * 4 + k, 1), :]
                    parts.append(jnp.concatenate([ek * p[:, 384 * a:384 * a + 384] for a in range(4)], axis=1))
                w = jnp.concatenate(parts, axis=0).astype(bf16)
                wscr[pl.ds(pl.multiple_of(t * 96 + pair * 48, 16), 48), :] = w
            return 0
        lax.fori_loop(0, TILES, wtile, 0, unroll=2)

        xscr[...] = jnp.dot(wscr[...], rt_ref[...], preferred_element_type=f32)

        ekt = ektscr[ch]

        for g in range(4):
            ep = []
            for h in range(2):
                evec = jnp.zeros((1, 128), f32)
                for k4 in range(4):
                    k = 8 * g + 4 * h + k4
                    p = kq_ref[ch * BLOCK + k]
                    pt = p // 4
                    pr = (pt % 32) * TILES + pt // 32
                    sh = (PITCH * (k4 + 4) - PITCH * (p % 4)) % 128
                    here = lane // PITCH == k4
                    e = pltpu.roll(tab[pt], sh, 1)
                    e = jnp.where(here, e, 0.0)
                    e = jnp.concatenate([e, jnp.zeros((8, 128), f32)], axis=0).astype(bf16)
                    bd[pl.ds(128 * h + PITCH * k4, PITCH), pl.ds(128 * h, 128)] = e
                    er = pltpu.roll(etab_ref[pl.ds(pr, 1), :], sh, 1)
                    evec = jnp.where(here, er, evec)
                ep.append(evec)
            for h in range(2):
                xs = [[None] * 4 for _ in range(2)]
                for k4 in range(4):
                    k = 8 * g + 4 * h + k4
                    for vt in range(2):
                        x = xscr[NB * k:NB * k + NB, 128 * vt:128 * vt + 128]
                        xs[vt][k4] = pltpu.roll(x, PITCH * k4, 1) if k4 else x
                for v in range(NV):
                    vt, s = VSLOT[v]
                    rel = (lane - NB * s + 128) % 128 // PITCH
                    y = xs[vt][3]
                    for k4 in range(3):
                        y = jnp.where(rel == k4, xs[vt][k4], y)
                    if s:
                        y = pltpu.roll(y, 128 - NB * s, 1)
                    ybuf[NB * v:NB * v + NB, 128 * h:128 * h + 128] = y
            z = jnp.dot(ybuf[...].astype(bf16), bd[...], preferred_element_type=f32)
            for h in range(2):
                t = 2 * g + h
                ek = jnp.zeros((NB, 128), f32)
                for k4 in range(4):
                    c = ekt[PITCH * k4:PITCH * k4 + NB, t:t + 1]
                    ek = jnp.where(lane // PITCH == k4, c, ek)
                diff = ep[h] - ek
                occ = jax.nn.sigmoid(ek * (-1.0 / KT)) - jax.nn.sigmoid(ep[h] * (-1.0 / KT))
                acc = jnp.zeros((NB, 128), f32)
                for v in range(NV):
                    zz = z[NB * v:NB * v + NB, 128 * h:128 * h + 128]
                    d = diff - freq_ref[v]
                    st = zz * zz * jnp.exp(d * d * (-1.0 / (2 * SIGMA * SIGMA)))
                    acc = acc + st
                    so = st * occ
                    phacc[v] += so[0:8] + so[8:16] + so[16:24]
                aescr[pl.ds(pl.multiple_of(ch * 4 * NB + NB * g, 8), NB), 128 * h:128 * h + 128] = acc
        return 0
    lax.fori_loop(0, 16, chunk, 0)
    sums = jnp.concatenate([jnp.sum(phacc[v], axis=0, keepdims=True) for v in range(NV)]
                           + [jnp.zeros((16 - NV, 128), f32)], axis=0)
    sums = jnp.sum(sums, axis=1, keepdims=True)
    phonon = jnp.where(lane == 96, sums[0:8], 0.0) + jnp.where(lane == 97, sums[8:16], 0.0)
    res = jnp.dot(aescr[...], fold, preferred_element_type=f32, precision=lax.Precision.HIGHEST)
    for ch in range(16):
        out = phonon
        for g in range(4):
            for t in range(3):
                a = 4 * NB * ch + NB * g + 8 * t
                piece = res[a:a + 8, :]
                sft = 32 * t + 8 * g
                out = out + (pltpu.roll(piece, sft, 1) if sft else piece)
        el_ref[ch] = out


def compute(core, kq, freq, phase, rt, eig, etab):
    f32, bf16 = jnp.float32, jnp.bfloat16
    smem = pl.BlockSpec(memory_space=pltpu.SMEM)
    vmem = pl.BlockSpec(memory_space=pltpu.VMEM)
    return pl.pallas_call(
        compute_kernel,
        out_shape=jax.ShapeDtypeStruct((16, 8, 128), f32),
        in_specs=[smem, smem, smem, vmem, vmem, vmem, vmem],
        out_specs=vmem,
        scratch_shapes=[
            pltpu.VMEM((256, NB, 128), f32),
            pltpu.VMEM((256, 128), f32),
            pltpu.VMEM((16 * BLOCK, NR * NB), f32),
            pltpu.VMEM((TILES * 128, 384), f32),
            pltpu.VMEM((16, 128, 8), f32),
            pltpu.VMEM((BLOCK * NB, NR * NB), bf16),
            pltpu.VMEM((BLOCK * NB, 256), f32),
            pltpu.VMEM((256, 256), bf16),
            pltpu.VMEM((NV * NB, 256), f32),
            pltpu.VMEM((64 * NB, 256), f32),
            pltpu.VMEM((NV, 8, 128), f32),
        ],
        compiler_params=pltpu.CompilerParams(vmem_limit_bytes=56 << 20),
        name="linewidths",
    )(core, kq, freq, phase, rt, eig, etab)


def place():
    ka, pb, row = lax.axis_index("ka"), lax.axis_index("pb"), lax.axis_index("row")
    return ka // 2, ka % 2, row, pb // 8, pb % 8


def device(y, core, x, y_lo, z):
    return {"ka": 2 * y + core, "pb": 8 * y_lo + z, "row": x}


def remote(src, dst, send, recv, target):
    return pltpu.make_async_remote_copy(src_ref=src, dst_ref=dst, send_sem=send, recv_sem=recv,
                                        device_id=target, device_id_type=pl.DeviceIdType.MESH)


def exchange_kernel(rs_ref, eg_ref, et_ref, rt_ref, eig_ref, etab_ref,
                    own, r_send, r_recv, t_send, t_recv, e_send, e_recv,
                    up_send, up_recv, dn_send, dn_recv,
                    rf_send, rf_recv, ef_send, ef_recv, tf_send, tf_recv):
    y, c, x, w, z = place()
    me = y * 4 + x
    partner = device(y, 1 - c, x, w, z)
    above = device(y, c, x, w, (z + 1) % 8)
    below = device(y, c, x, w, (z + 7) % 8)
    others = []
    for d in range(1, 16):
        yy, xx = (y + d // 4) % 4, (x + d % 4) % 4
        others.append((yy, xx, device(yy, c, xx, w, z)))

    barrier = pltpu.get_barrier_semaphore()
    for target in [o[2] for o in others] + [partner, above, below]:
        pl.semaphore_signal(barrier, inc=1, device_id=target, device_id_type=pl.DeviceIdType.MESH)
    pl.semaphore_wait(barrier, 18)

    copies = []
    locals_ = [
        pltpu.make_async_copy(eg_ref.at[z], eig_ref.at[z, c, me], own.at[0]),
        pltpu.make_async_copy(et_ref, etab_ref.at[c, me], own.at[1]),
        pltpu.make_async_copy(rs_ref.at[y, x], rt_ref.at[c, y, x], own.at[2]),
    ]
    for cp in locals_:
        cp.start()
    for n, (yy, xx, target) in enumerate(others):
        cp = remote(eg_ref.at[z], eig_ref.at[z, c, me], e_send.at[n], e_recv.at[n], target)
        cp.start()
        copies.append(cp)
    for n, (yy, xx, target) in enumerate(others):
        cp = remote(et_ref, etab_ref.at[c, me], t_send.at[n], t_recv.at[n], target)
        cp.start()
        copies.append(cp)
    for n, (yy, xx, target) in enumerate(others):
        cp = remote(rs_ref.at[yy, xx], rt_ref.at[c, y, x], r_send.at[n], r_recv.at[n], target)
        cp.start()
        copies.append(cp)

    def arrival(ref, recv):
        pltpu.make_async_copy(ref, ref, recv).wait()

    locals_[0].wait()
    for n in range(15):
        yy, xx = (y + 16 - (n + 1) // 4) % 4, (x + 16 - (n + 1) % 4) % 4
        arrival(eig_ref.at[z, c, yy * 4 + xx], e_recv.at[n])
    for step in range(4):
        for part in range(4):
            if step:
                arrival(eig_ref.at[(z + 8 - step) % 8, c, pl.ds(4 * part, 4)], up_recv.at[step - 1, part])
            src = eig_ref.at[(z + 8 - step) % 8, c, pl.ds(4 * part, 4)]
            cp = remote(src, src, up_send.at[step, part], up_recv.at[step, part], above)
            cp.start()
            copies.append(cp)
            if step < 3 or step == 3:
                if step:
                    arrival(eig_ref.at[(z + step) % 8, c, pl.ds(4 * part, 4)], dn_recv.at[step - 1, part])
                if step < 3:
                    src = eig_ref.at[(z + step) % 8, c, pl.ds(4 * part, 4)]
                    cp = remote(src, src, dn_send.at[step, part], dn_recv.at[step, part], below)
                    cp.start()
                    copies.append(cp)
        done = [(z + 8 - step) % 8] if step == 0 else [(z + 8 - step) % 8, (z + step) % 8]
        for m, t in enumerate(done):
            f = step if m == 0 else 4 + step
            cp = remote(eig_ref.at[t, c], eig_ref.at[t, c], ef_send.at[f], ef_recv.at[f], partner)
            cp.start()
            copies.append(cp)
    locals_[1].wait()
    for n in range(15):
        yy, xx = (y + 16 - (n + 1) // 4) % 4, (x + 16 - (n + 1) % 4) % 4
        arrival(etab_ref.at[c, yy * 4 + xx], t_recv.at[n])
    cp = remote(etab_ref.at[c], etab_ref.at[c], tf_send.at[0], tf_recv.at[0], partner)
    cp.start()
    copies.append(cp)
    locals_[2].wait()
    for dy in range(4):
        yy = (y + 4 - dy) % 4
        for dx in range(4):
            n = 4 * dy + dx - 1
            if n >= 0:
                arrival(rt_ref.at[c, yy, (x + 4 - dx) % 4], r_recv.at[n])
        cp = remote(rt_ref.at[c, yy], rt_ref.at[c, yy], rf_send.at[dy], rf_recv.at[dy], partner)
        cp.start()
        copies.append(cp)
    for part in range(4):
        arrival(eig_ref.at[(z + 4) % 8, c, pl.ds(4 * part, 4)], up_recv.at[3, part])
    cp = remote(eig_ref.at[(z + 4) % 8, c], eig_ref.at[(z + 4) % 8, c], ef_send.at[4], ef_recv.at[4], partner)
    cp.start()
    copies.append(cp)
    for f in range(8):
        t = (z + 8 - f) % 8 if f < 5 else (z + f - 4) % 8
        arrival(eig_ref.at[t, 1 - c], ef_recv.at[f])
    arrival(etab_ref.at[1 - c], tf_recv.at[0])
    for dy in range(4):
        arrival(rt_ref.at[1 - c, (y + 4 - dy) % 4], rf_recv.at[dy])
    for cp in copies:
        cp.wait_send()


def exchange(rs, eg, et):
    vmem = pl.BlockSpec(memory_space=pltpu.VMEM)
    dma = pltpu.SemaphoreType.DMA
    return pl.pallas_call(
        exchange_kernel,
        out_shape=(jax.ShapeDtypeStruct((2, 4, 4, 48, 256), jnp.bfloat16),
                   jax.ShapeDtypeStruct((8, 2, 16, NB, 128), jnp.bfloat16),
                   jax.ShapeDtypeStruct((2, 16, 8, 128), jnp.float32)),
        in_specs=[vmem] * 3,
        out_specs=(vmem,) * 3,
        scratch_shapes=[dma((3,)), dma((15,)), dma((15,)), dma((15,)), dma((15,)), dma((15,)), dma((15,)),
                        dma((4, 4)), dma((4, 4)), dma((3, 4)), dma((3, 4)),
                        dma((4,)), dma((4,)), dma((8,)), dma((8,)), dma((1,)), dma((1,))],
        compiler_params=pltpu.CompilerParams(collective_id=0, has_side_effects=True),
        name="exchange",
    )(rs, eg, et)


def reduce_kernel(el_ref, out_ref, got, mine, peers, half, own, a_send, a_recv, b_send, b_recv, p_send, p_recv):
    f32 = jnp.float32
    y, c, x, w, z = place()
    me = y * 4 + x
    partner = device(y, 1 - c, x, w, z)
    plane, column = [], []
    for d in range(1, 16):
        yy, xx = (y + d // 4) % 4, (x + d % 4) % 4
        plane.append((yy * 4 + xx, device(yy, c, xx, w, z)))
        ww, zz = (w + d // 8) % 2, (z + d % 8) % 8
        column.append((ww * 8 + zz, device(y, c, x, ww, zz)))
    barrier = pltpu.get_barrier_semaphore()
    for target in [o[1] for o in plane + column] + [partner]:
        pl.semaphore_signal(barrier, inc=1, device_id=target, device_id_type=pl.DeviceIdType.MESH)
    pl.semaphore_wait(barrier, 31)

    copies = []
    for n, (block, target) in enumerate(plane):
        cp = remote(el_ref.at[block], got.at[me], a_send.at[n], a_recv.at[n], target)
        cp.start()
        copies.append(cp)
    cp = pltpu.make_async_copy(el_ref.at[me], got.at[me], own.at[0])
    cp.start()
    cp.wait()
    for n in range(15):
        yy, xx = (y + 16 - (n + 1) // 4) % 4, (x + 16 - (n + 1) % 4) % 4
        ref = got.at[yy * 4 + xx]
        pltpu.make_async_copy(ref, ref, a_recv.at[n]).wait()
    lane = lax.broadcasted_iota(jnp.int32, (8, 128), 1)
    total = jnp.zeros((8, 128), f32)
    phonon = jnp.zeros((8, 128), f32)
    for s in range(16):
        tile = got[s]
        total = total + tile
        phonon = phonon + pltpu.roll(jnp.where((lane == 96) | (lane == 97), tile, 0.0), (2 * s + 32) % 128, 1)
    mine[...] = total
    half[0] = phonon
    for n, (block, target) in enumerate(column):
        cp = remote(mine, peers.at[w * 8 + z], b_send.at[n], b_recv.at[n], target)
        cp.start()
        copies.append(cp)
    cp = remote(half.at[0], half.at[1], p_send.at[0], p_recv.at[0], partner)
    cp.start()
    copies.append(cp)
    for n in range(15):
        ww, zz = (w + 2 - (n + 1) // 8) % 2, (z + 16 - (n + 1) % 8) % 8
        ref = peers.at[ww * 8 + zz]
        pltpu.make_async_copy(ref, ref, b_recv.at[n]).wait()
    pltpu.make_async_copy(half.at[1], half.at[1], p_recv.at[0]).wait()
    acc = jnp.zeros((8, 128), f32)
    for s in range(16):
        acc = acc + jnp.where(s == w * 8 + z, total, peers[s])
    out_ref[0] = acc
    out_ref[1] = half[0] + half[1]
    for cp in copies:
        cp.wait_send()


def reduce(el):
    f32 = jnp.float32
    vmem = pl.BlockSpec(memory_space=pltpu.VMEM)
    dma = pltpu.SemaphoreType.DMA
    return pl.pallas_call(
        reduce_kernel,
        out_shape=jax.ShapeDtypeStruct((2, 8, 128), f32),
        in_specs=[vmem],
        out_specs=vmem,
        scratch_shapes=[pltpu.VMEM((16, 8, 128), f32), pltpu.VMEM((8, 128), f32), pltpu.VMEM((16, 8, 128), f32),
                        pltpu.VMEM((2, 8, 128), f32),
                        dma((1,)), dma((15,)), dma((15,)), dma((15,)), dma((15,)), dma((1,)), dma((1,))],
        compiler_params=pltpu.CompilerParams(collective_id=1, has_side_effects=True),
        name="reduce",
    )(el)


def phase_table(lattice, kpoint_rows):
    rvec = lattice.astype(jnp.float32)
    argument = (
        rvec[:, 0:1] * kpoint_rows[:, 0][None, :]
        + rvec[:, 1:2] * kpoint_rows[:, 1][None, :]
        + rvec[:, 2:3] * kpoint_rows[:, 2][None, :]
    )
    return jnp.cos(2.0 * math.pi * argument).astype(jnp.bfloat16)


def on_device(coupling, rotation, freq, eigvec, energies, window, kq_index, kpoints, lattice):
    f32, bf16 = jnp.float32, jnp.bfloat16
    y, c, x, w, z = place()
    coup = coupling.reshape(4, 2, NM, NB, NB)
    rotated = jnp.einsum("qrcij,qcv->qrvij", coup, rotation, preferred_element_type=f32).astype(bf16)
    rs = rotated.reshape(4, 2, 4, NV, NB, NB).transpose(0, 2, 1, 5, 3, 4).reshape(4, 4, 48, NV, NB)
    low = jnp.pad(rs[:, :, :, :5].reshape(4, 4, 48, 120), ((0, 0), (0, 0), (0, 0), (0, 8)))
    high = jnp.pad(rs[:, :, :, 5:].reshape(4, 4, 48, 96), ((0, 0), (0, 0), (0, 0), (0, 32)))
    rs = jnp.concatenate([low, high], axis=-1)
    eg = jnp.pad(eigvec.reshape(8, 4, NB, NB), ((0, 0), (0, 0), (0, 0), (0, 8)))
    eg = eg.transpose(0, 2, 1, 3).reshape(8, NB, 128)
    et = jnp.concatenate([energies, window.astype(f32)[:, None], jnp.zeros((32, 7), f32)], axis=1).reshape(8, 128)
    rt, eig, etab = exchange(rs, eg, et)

    lat = lattice.reshape(4, 2, 4, 2, 3).transpose(1, 0, 2, 3, 4).reshape(NR, 3)
    kp = lax.dynamic_index_in_dim(kpoints.reshape(4, 2, 128, 3), c, 1, keepdims=False).reshape(512, 3)
    phase = phase_table(lat, kp).T
    kq = lax.dynamic_index_in_dim(kq_index.reshape(4, 4, 2, 128), y, 0, keepdims=False)
    kq = lax.dynamic_index_in_dim(kq, c, 1, keepdims=False).reshape(512)
    slot = ((kq // 4) % 8) * 32 + ((kq // 128) % 2) * 16 + (kq // 256) * 4 + (kq // 32) % 4
    kq = slot * 4 + kq % 4
    fr = lax.dynamic_slice(freq, (y, NV * x), (1, NV)).reshape(NV)
    el = compute(c.reshape(1).astype(jnp.int32), kq, fr, phase, rt.reshape(NR * NB, 256),
                 eig.reshape(256, NB, 128), etab.reshape(256, 128))
    out = reduce(el)
    norm = 1.0 / (math.sqrt(2.0 * math.pi) * SIGMA)
    electron = out[0, :, :96].reshape(8, 3, 32).transpose(2, 1, 0).reshape(32, NB) * (norm / 55296.0)
    phonon = out[1, :, :32].reshape(8, 16, 2).transpose(1, 2, 0).reshape(16, 16)[:, :NV].reshape(4, NM) * (norm / 24576.0)
    return electron, phonon


def solution(mesh):
    return jax.shard_map(
        on_device,
        mesh=mesh,
        in_specs=(
            P("pb", ("ka", "row"), None),
            P("pb", None, None),
            P("pb", None),
            P(("ka", "row"), None, None),
            P(("ka", "row"), None),
            P(("ka", "row")),
            P("pb", None),
            P(),
            P(),
        ),
        out_specs=(P(("ka", "row"), None), P("pb", None)),
        check_vma=False,
    )
```

```python
import math

import jax
import jax.numpy as jnp
from jax import lax
from jax.experimental import pallas as pl
from jax.experimental.pallas import tpu as pltpu
from jax.sharding import PartitionSpec as P

SIGMA = 0.1
KT = 0.2
NB, NM, NR = 24, 36, 64
NV = 9
PITCH = 32
VSLOT = [(v // 5, v % 5) for v in range(NV)]


def constants():
    f32, bf16 = jnp.float32, jnp.bfloat16
    r1 = lax.broadcasted_iota(jnp.int32, (NB, 384), 0)
    c1 = lax.broadcasted_iota(jnp.int32, (NB, 384), 1)
    spread = jnp.where(c1 % NB == r1, 1.0, 0.0).astype(bf16)
    r2 = lax.broadcasted_iota(jnp.int32, (NR, NR * NB), 0)
    c2 = lax.broadcasted_iota(jnp.int32, (NR, NR * NB), 1)
    widen = jnp.where(c2 // NB == r2, 1.0, 0.0).astype(bf16)
    return spread, widen


def right_stage(t, c, rt_ref, eig_ref, spread, pscr, etscr, wbufs, xscr):
    f32, bf16 = jnp.float32, jnp.bfloat16
    tt = jnp.concatenate([eig_ref[32 * t + 16 * c + b] for b in range(16)], axis=1)
    etscr[...] = lax.dot_general(tt, spread, (((0,), (0,)), ((), ())), preferred_element_type=f32)
    for sub in range(4):
        wbuf = wbufs[sub % 2]
        for pair in range(8):
            parts = []
            for kk in range(2):
                k = 16 * sub + 2 * pair + kk
                ek = etscr[PITCH * k:PITCH * k + NB, :]
                p = pscr[pl.ds((k // 4) * 32 + 4 * t + k % 4, 1), :]
                parts.append(jnp.concatenate([ek * p[:, 384 * a:384 * a + 384] for a in range(4)], axis=1))
            wbuf[48 * pair:48 * pair + 48, :] = jnp.concatenate(parts, axis=0).astype(bf16)
        xscr[t, 384 * sub:384 * sub + 384, :] = jnp.dot(wbuf[...], rt_ref[...].reshape(NR * NB, 256), preferred_element_type=f32)


def final_stage(t, c, q, vq, kq_ref, freq_ref, eig_ref, etab_ref, xscr, bds, ybufs, aes, phacc, acc_ref):
    f32, bf16 = jnp.float32, jnp.bfloat16
    lane = lax.broadcasted_iota(jnp.int32, (1, 128), 1)
    ekt = jnp.transpose(etab_ref[pl.ds(pl.multiple_of(32 * t + 16 * c, 16), 16), :])
    for g in range(8):
        bd, ybuf = bds.at[g % 4], ybufs.at[g % 4]
        eps = []
        for h in range(2):
            b = 2 * g + h
            evec = jnp.zeros((1, 128), f32)
            for k4 in range(4):
                p = kq_ref[q, 4 * t + c * 128 + (b // 4) * 256 + (b % 4) * 32 + k4]
                tile = ((p >> 2) & 7) * 32 + ((p >> 7) & 1) * 16 + ((p >> 8) << 2) + ((p >> 5) & 3)
                sh = ((k4 - p) & 3) * PITCH
                here = lane // PITCH == k4
                e = pltpu.roll(eig_ref[tile].astype(f32), sh, 1)
                e = jnp.where(here, e, 0.0)
                e = jnp.concatenate([e, jnp.zeros((8, 128), f32)], axis=0).astype(bf16)
                bd[128 * h + PITCH * k4:128 * h + PITCH * k4 + PITCH, 128 * h:128 * h + 128] = e
                er = pltpu.roll(etab_ref[pl.ds(tile, 1), :], sh, 1)
                evec = jnp.where(here, er, evec)
            eps.append(evec)
        for h in range(2):
            xs = [[None] * 4 for _ in range(2)]
            for k4 in range(4):
                k = 8 * g + 4 * h + k4
                for vt in range(2):
                    x = xscr[t, NB * k:NB * k + NB, 128 * vt:128 * vt + 128]
                    xs[vt][k4] = pltpu.roll(x, PITCH * k4, 1) if k4 else x
            for v in range(NV):
                vt, s = VSLOT[v]
                rel = (lane - NB * s + 128) % 128 // PITCH
                yv = xs[vt][3]
                for k4 in range(3):
                    yv = jnp.where(rel == k4, xs[vt][k4], yv)
                if s:
                    yv = pltpu.roll(yv, 128 - NB * s, 1)
                ybuf[NB * v:NB * v + NB, 128 * h:128 * h + 128] = yv
        zz = jnp.dot(ybuf[...].astype(bf16), bd[...], preferred_element_type=f32)
        for h in range(2):
            b = 2 * g + h
            ek = jnp.zeros((NB, 128), f32)
            for k4 in range(4):
                ek = jnp.where(lane // PITCH == k4, ekt[PITCH * k4:PITCH * k4 + NB, b:b + 1], ek)
            diff = eps[h] - ek
            occ = jax.nn.sigmoid(ek * (-1.0 / KT)) - jax.nn.sigmoid(eps[h] * (-1.0 / KT))
            acc = jnp.zeros((NB, 128), f32)
            for v in range(NV):
                zv = zz[NB * v:NB * v + NB, 128 * h:128 * h + 128]
                d = diff - freq_ref[q, NV * vq + v]
                st = zv * zv * jnp.exp(d * d * (-1.0 / (2 * SIGMA * SIGMA)))
                acc = acc + st
                so = st * occ
                phacc[v] += so[0:8] + so[8:16] + so[16:24]
            aes[NB * g:NB * g + NB, 128 * h:128 * h + 128] = acc
    r3 = lax.broadcasted_iota(jnp.int32, (256, 128), 0)
    c3 = lax.broadcasted_iota(jnp.int32, (256, 128), 1)
    fold = jnp.where(c3 == (r3 // 128) * 64 + 4 * t + (r3 % 128) // PITCH, 1.0, 0.0).astype(f32)
    acc_ref[...] += jnp.dot(aes[...], fold, preferred_element_type=f32, precision=lax.Precision.HIGHEST)


def pack_sums(phacc, acc_ref, el_ref):
    f32 = jnp.float32
    lane = lax.broadcasted_iota(jnp.int32, (1, 128), 1)
    sums = jnp.concatenate([jnp.sum(phacc[v], axis=0, keepdims=True) for v in range(NV)]
                           + [jnp.zeros((16 - NV, 128), f32)], axis=0)
    sums = jnp.sum(sums, axis=1, keepdims=True)
    phonon = jnp.where(lane == 96, sums[0:8], 0.0) + jnp.where(lane == 97, sums[8:16], 0.0)
    for b in range(16):
        out = phonon
        for u in range(3):
            a = NB * (b // 2) + 8 * u
            piece = jnp.where(lane // 64 == b % 2, acc_ref[a:a + 8, :], 0.0)
            shift = (32 * u + 64 * (b % 2)) % 128
            out = out + (pltpu.roll(piece, shift, 1) if shift else piece)
        el_ref[b] = out


def place():
    ka, pb, row = lax.axis_index("ka"), lax.axis_index("pb"), lax.axis_index("row")
    return ka // 2, ka % 2, row, pb // 8, pb % 8


def device(y, core, x, y_lo, z):
    return {"ka": 2 * y + core, "pb": 8 * y_lo + z, "row": x}


def phases(y_unused, c, kp_ref, lat_ref, widen, pscr):
    f32 = jnp.float32
    lat = lat_ref[...].astype(f32)
    for u in range(4):
        cols = pl.ds(pl.multiple_of(256 * u + 128 * c, 128), 128)
        arg = (lat[:, 0:1] * kp_ref[0:1, cols] + lat[:, 1:2] * kp_ref[1:2, cols]
               + lat[:, 2:3] * kp_ref[2:3, cols])
        ph = jnp.cos(2.0 * math.pi * arg).astype(jnp.bfloat16)
        pscr[128 * u:128 * u + 128, :] = lax.dot_general(
            ph, widen, (((0,), (0,)), ((), ())), preferred_element_type=f32)


def mega_kernel(kq_ref, freq_ref, kp_ref, lat_ref, rs_ref, eg_ref, et_ref, out_ref,
                rt, eig, etab, pscr, etscr, wa, wb, xscr, bds, ybufs, aes, phacc, acc_ref,
                el, got, mine, peers, half,
                own, r_send, r_recv, t_send, t_recv, e_send, e_recv,
                up_send, up_recv, dn_send, dn_recv, ut_send, ut_recv, dt_send, dt_recv,
                rf_send, rf_recv, ef_send, ef_recv, tf_send, tf_recv,
                a_send, a_recv, b_send, b_recv, p_send, p_recv):
    f32 = jnp.float32
    y, c, x, w, z = place()
    me = y * 4 + x
    partner = device(y, 1 - c, x, w, z)
    above = device(y, c, x, w, (z + 1) % 8)
    below = device(y, c, x, w, (z + 7) % 8)
    plane, column = [], []
    for d in range(1, 16):
        yy, xx = (y + d // 4) % 4, (x + d % 4) % 4
        plane.append((yy, xx, device(yy, c, xx, w, z)))
        ww, zz = (w + d // 8) % 2, (z + d % 8) % 8
        column.append(device(y, c, x, ww, zz))

    barrier = pltpu.get_barrier_semaphore()
    for target in [o[2] for o in plane] + column + [partner]:
        pl.semaphore_signal(barrier, inc=1, device_id=target, device_id_type=pl.DeviceIdType.MESH)

    local = [
        pltpu.make_async_copy(eg_ref.at[z], eig.at[32 * z + 16 * c + me], own.at[0]),
        pltpu.make_async_copy(et_ref.at[pl.ds(z, 1)], etab.at[pl.ds(32 * z + 16 * c + me, 1)], own.at[1]),
        pltpu.make_async_copy(rs_ref.at[y, x], rt.at[y, c, x], own.at[2]),
    ]
    for cp in local:
        cp.start()
    pl.semaphore_wait(barrier, 31)

    copies = []

    def send(src, dst, s, r, target):
        cp = pltpu.make_async_remote_copy(src_ref=src, dst_ref=dst, send_sem=s, recv_sem=r, device_id=target,
                                          device_id_type=pl.DeviceIdType.MESH)
        cp.start()
        return cp

    def arrival(ref, recv):
        pltpu.make_async_copy(ref, ref, recv).wait()

    def tiles(t, core):
        return eig.at[pl.ds(32 * t + 16 * core, 16)]

    def rows(t, core):
        return etab.at[pl.ds(pl.multiple_of(32 * t + 16 * core, 16), 16)]

    here = 32 * z + 16 * c + me
    for n, (yy, xx, target) in enumerate(plane):
        copies.append(send(eg_ref.at[z], eig.at[here], e_send.at[n], e_recv.at[n], target))
        copies.append(send(et_ref.at[pl.ds(z, 1)], etab.at[pl.ds(here, 1)], t_send.at[n], t_recv.at[n], target))
    for n, (yy, xx, target) in enumerate(plane):
        copies.append(send(rs_ref.at[yy, xx], rt.at[y, c, x], r_send.at[n], r_recv.at[n], target))

    spread, widen = constants()
    phases(y, c, kp_ref, lat_ref, widen, pscr)
    bds[...] = jnp.zeros_like(bds)
    phacc[...] = jnp.zeros_like(phacc)
    acc_ref[...] = jnp.zeros_like(acc_ref)

    def ring(step):
        up, dn = (z + 8 - step) % 8, (z + step) % 8
        if step:
            arrival(tiles(up, c), up_recv.at[step - 1])
            arrival(rows(up, c), ut_recv.at[step - 1])
        if step < 4:
            send(tiles(up, c), tiles(up, c), up_send.at[step], up_recv.at[step], above)
            send(rows(up, c), rows(up, c), ut_send.at[step], ut_recv.at[step], above)
        if 0 < step < 4:
            arrival(tiles(dn, c), dn_recv.at[step - 1])
            arrival(rows(dn, c), dt_recv.at[step - 1])
        if step < 3:
            send(tiles(dn, c), tiles(dn, c), dn_send.at[step], dn_recv.at[step], below)
            send(rows(dn, c), rows(dn, c), dt_send.at[step], dt_recv.at[step], below)
        for f, t in [(step, up)] + ([(4 + step, dn)] if 0 < step < 4 else []):
            send(tiles(t, c), tiles(t, c), ef_send.at[f], ef_recv.at[f], partner)
            send(rows(t, c), rows(t, c), tf_send.at[f], tf_recv.at[f], partner)

    def slice_of(f):
        return (z + 8 - f) % 8 if f < 5 else (z + f - 4) % 8

    for cp in local:
        cp.wait()
    for n in range(15):
        d = n + 1
        b = (y + 4 - d // 4) % 4 * 4 + (x + 4 - d % 4) % 4
        arrival(eig.at[32 * z + 16 * c + b], e_recv.at[n])
        arrival(etab.at[pl.ds(32 * z + 16 * c + b, 1)], t_recv.at[n])
    ring(0)
    ring(1)
    for dy in range(4):
        yy = (y + 4 - dy) % 4
        for dx in range(4):
            if dy or dx:
                arrival(rt.at[yy, c, (x + 4 - dx) % 4], r_recv.at[4 * dy + dx - 1])
        copies.append(send(rt.at[yy, c], rt.at[yy, c], rf_send.at[dy], rf_recv.at[dy], partner))
    for dy in range(4):
        arrival(rt.at[(y + 4 - dy) % 4, 1 - c], rf_recv.at[dy])

    def right(i, _):
        for step, at in ((2, 1), (3, 3), (4, 5)):
            pl.when(i == at)(lambda step=step: ring(step))
        t = (z + 8 + (1 - 2 * (i % 2)) * ((i + 1) // 2)) % 8
        right_stage(t, c, rt, eig, spread, pscr, etscr, (wa, wb), xscr)
        return 0
    lax.fori_loop(0, 8, right, 0)

    for f in range(8):
        arrival(tiles(slice_of(f), 1 - c), ef_recv.at[f])
        arrival(rows(slice_of(f), 1 - c), tf_recv.at[f])

    def final(t, _):
        final_stage(t, c, y, x, kq_ref, freq_ref, eig, etab, xscr, bds, ybufs, aes, phacc, acc_ref)
        return 0
    lax.fori_loop(0, 8, final, 0)
    pack_sums(phacc, acc_ref, el)

    for n, (yy, xx, target) in enumerate(plane):
        copies.append(send(el.at[yy * 4 + xx], got.at[me], a_send.at[n], a_recv.at[n], target))
    for n in range(15):
        d = n + 1
        arrival(got.at[(y + 4 - d // 4) % 4 * 4 + (x + 4 - d % 4) % 4], a_recv.at[n])
    lane = lax.broadcasted_iota(jnp.int32, (8, 128), 1)
    total = jnp.zeros((8, 128), f32)
    phonon = jnp.zeros((8, 128), f32)
    for s in range(16):
        tile = jnp.where(me == s, el[s], got[s])
        total = total + tile
        phonon = phonon + pltpu.roll(jnp.where((lane == 96) | (lane == 97), tile, 0.0), (2 * s + 32) % 128, 1)
    mine[...] = total
    half[0] = phonon
    for n, target in enumerate(column):
        copies.append(send(mine, peers.at[w * 8 + z], b_send.at[n], b_recv.at[n], target))
    copies.append(send(half.at[0], half.at[1], p_send.at[0], p_recv.at[0], partner))
    for n in range(15):
        d = n + 1
        arrival(peers.at[(w + 2 - d // 8) % 2 * 8 + (z + 8 - d % 8) % 8], b_recv.at[n])
    arrival(half.at[1], p_recv.at[0])
    acc = jnp.zeros((8, 128), f32)
    for s in range(16):
        acc = acc + jnp.where(w * 8 + z == s, total, peers[s])
    out_ref[0] = acc
    out_ref[1] = half[0] + half[1]

    for cp in copies:
        cp.wait_send()
    for step in range(4):
        arrival(tiles(z, c), up_send.at[step])
        arrival(rows(z, c), ut_send.at[step])
        if step < 3:
            arrival(tiles(z, c), dn_send.at[step])
            arrival(rows(z, c), dt_send.at[step])
    for f in range(8):
        arrival(tiles(z, c), ef_send.at[f])
        arrival(rows(z, c), tf_send.at[f])


def mega(kq, freq, kp, lat, rs, eg, et):
    f32, bf16 = jnp.float32, jnp.bfloat16
    smem = pl.BlockSpec(memory_space=pltpu.SMEM)
    vmem = pl.BlockSpec(memory_space=pltpu.VMEM)
    dma = pltpu.SemaphoreType.DMA
    return pl.pallas_call(
        mega_kernel,
        out_shape=jax.ShapeDtypeStruct((2, 8, 128), f32),
        in_specs=[smem, smem] + [vmem] * 5,
        out_specs=vmem,
        scratch_shapes=[
            pltpu.VMEM((4, 2, 4, 48, 256), bf16), pltpu.VMEM((256, NB, 128), bf16), pltpu.VMEM((256, 128), f32),
            pltpu.VMEM((512, NR * NB), f32), pltpu.VMEM((2048, 384), f32),
            pltpu.VMEM((384, NR * NB), bf16), pltpu.VMEM((384, NR * NB), bf16), pltpu.VMEM((8, 1536, 256), f32),
            pltpu.VMEM((4, 256, 256), bf16), pltpu.VMEM((4, NV * NB, 256), f32), pltpu.VMEM((8 * NB, 256), f32),
            pltpu.VMEM((NV, 8, 128), f32), pltpu.VMEM((8 * NB, 128), f32),
            pltpu.VMEM((16, 8, 128), f32), pltpu.VMEM((16, 8, 128), f32), pltpu.VMEM((8, 128), f32),
            pltpu.VMEM((16, 8, 128), f32), pltpu.VMEM((2, 8, 128), f32),
            dma((3,)), dma((15,)), dma((15,)), dma((15,)), dma((15,)), dma((15,)), dma((15,)),
            dma((4,)), dma((4,)), dma((3,)), dma((3,)), dma((4,)), dma((4,)), dma((3,)), dma((3,)),
            dma((4,)), dma((4,)), dma((8,)), dma((8,)), dma((8,)), dma((8,)),
            dma((15,)), dma((15,)), dma((15,)), dma((15,)), dma((1,)), dma((1,))],
        compiler_params=pltpu.CompilerParams(collective_id=0, has_side_effects=True, vmem_limit_bytes=60 << 20),
        name="linewidths",
    )(kq, freq, kp, lat, rs, eg, et)


def on_device(coupling, rotation, freq, eigvec, energies, window, kq_index, kpoints, lattice):
    f32, bf16 = jnp.float32, jnp.bfloat16
    coup = coupling.reshape(4, 2, NM, NB, NB)
    rotated = jnp.einsum("qrcij,qcv->qrvij", coup, rotation, preferred_element_type=f32).astype(bf16)
    rs = rotated.reshape(4, 2, 4, NV, NB, NB).transpose(0, 2, 1, 5, 3, 4).reshape(4, 4, 48, NV, NB)
    low = jnp.pad(rs[:, :, :, :5].reshape(4, 4, 48, 120), ((0, 0), (0, 0), (0, 0), (0, 8)))
    high = jnp.pad(rs[:, :, :, 5:].reshape(4, 4, 48, 96), ((0, 0), (0, 0), (0, 0), (0, 32)))
    rs = jnp.concatenate([low, high], axis=-1)
    inside = jnp.arange(NB)[None, None, :] < window[:, None, None]
    eg = jnp.pad(jnp.where(inside, eigvec, jnp.zeros((), bf16)).reshape(8, 4, NB, NB), ((0, 0), (0, 0), (0, 0), (0, 8)))
    eg = eg.transpose(0, 2, 1, 3).reshape(8, NB, 128)
    et = jnp.pad(energies, ((0, 0), (0, 8))).reshape(8, 128)
    out = mega(kq_index, freq, kpoints.T, lattice, rs, eg, et)
    norm = 1.0 / (math.sqrt(2.0 * math.pi) * SIGMA)
    electron = out[0, :, :96].reshape(8, 3, 32).transpose(2, 1, 0).reshape(32, NB) * (norm / 55296.0)
    phonon = out[1, :, :32].reshape(8, 16, 2).transpose(1, 2, 0).reshape(16, 16)[:, :NV].reshape(4, NM) * (norm / 24576.0)
    return electron, phonon


def solution(mesh):
    return jax.shard_map(
        on_device,
        mesh=mesh,
        in_specs=(
            P("pb", ("ka", "row"), None),
            P("pb", None, None),
            P("pb", None),
            P(("ka", "row"), None, None),
            P(("ka", "row"), None),
            P(("ka", "row")),
            P("pb", None),
            P(),
            P(),
        ),
        out_specs=(P(("ka", "row"), None), P("pb", None)),
        check_vma=False,
    )
```

```python
import math

import jax
import jax.numpy as jnp
from jax import lax
from jax.experimental import pallas as pl
from jax.experimental.pallas import tpu as pltpu
from jax.sharding import PartitionSpec as P

SIGMA = 0.1
KT = 0.2
NB, NM, NR = 24, 36, 64
NV = 9
PITCH = 32
VSLOT = [(v // 5, v % 5) for v in range(NV)]


def constants():
    f32, bf16 = jnp.float32, jnp.bfloat16
    r1 = lax.broadcasted_iota(jnp.int32, (NB, 384), 0)
    c1 = lax.broadcasted_iota(jnp.int32, (NB, 384), 1)
    spread = jnp.where(c1 % NB == r1, 1.0, 0.0).astype(bf16)
    r2 = lax.broadcasted_iota(jnp.int32, (NR, NR * NB), 0)
    c2 = lax.broadcasted_iota(jnp.int32, (NR, NR * NB), 1)
    widen = jnp.where(c2 // NB == r2, 1.0, 0.0).astype(bf16)
    return spread, widen


def right_stage(t, c, rt_ref, eig_ref, spread, pscr, etscr, wbufs, xscr):
    f32, bf16 = jnp.float32, jnp.bfloat16
    tt = jnp.concatenate([eig_ref[32 * t + 16 * c + b] for b in range(16)], axis=1)
    etscr[...] = lax.dot_general(tt, spread, (((0,), (0,)), ((), ())), preferred_element_type=f32)
    for sub in range(4):
        wbuf = wbufs[sub % 2]
        for pair in range(8):
            parts = []
            for kk in range(2):
                k = 16 * sub + 2 * pair + kk
                ek = etscr[PITCH * k:PITCH * k + NB, :]
                p = pscr[pl.ds((k // 4) * 32 + 4 * t + k % 4, 1), :]
                parts.append(jnp.concatenate([ek * p[:, 384 * a:384 * a + 384] for a in range(4)], axis=1))
            wbuf[48 * pair:48 * pair + 48, :] = jnp.concatenate(parts, axis=0).astype(bf16)
        xscr[t, 384 * sub:384 * sub + 384, :] = jnp.dot(wbuf[...], rt_ref[...].reshape(NR * NB, 256), preferred_element_type=f32)


def final_stage(t, c, q, vq, kq_ref, freq_ref, eig_ref, etab_ref, xscr, bds, ybufs, aes, phacc, acc_ref):
    f32, bf16 = jnp.float32, jnp.bfloat16
    lane = lax.broadcasted_iota(jnp.int32, (1, 128), 1)
    ekt = jnp.transpose(etab_ref[pl.ds(pl.multiple_of(32 * t + 16 * c, 16), 16), :])
    for g in range(8):
        bd, ybuf = bds.at[g % 4], ybufs.at[g % 4]
        eps = []
        for h in range(2):
            b = 2 * g + h
            evec = jnp.zeros((1, 128), f32)
            for k4 in range(4):
                p = kq_ref[q, 4 * t + c * 128 + (b // 4) * 256 + (b % 4) * 32 + k4]
                tile = ((p >> 2) & 7) * 32 + ((p >> 7) & 1) * 16 + ((p >> 8) << 2) + ((p >> 5) & 3)
                sh = ((k4 - p) & 3) * PITCH
                here = lane // PITCH == k4
                e = pltpu.roll(eig_ref[tile].astype(f32), sh, 1)
                e = jnp.where(here, e, 0.0)
                e = jnp.concatenate([e, jnp.zeros((8, 128), f32)], axis=0).astype(bf16)
                bd[128 * h + PITCH * k4:128 * h + PITCH * k4 + PITCH, 128 * h:128 * h + 128] = e
                er = pltpu.roll(etab_ref[pl.ds(tile, 1), :], sh, 1)
                evec = jnp.where(here, er, evec)
            eps.append(evec)
        for h in range(2):
            xs = [[None] * 4 for _ in range(2)]
            for k4 in range(4):
                k = 8 * g + 4 * h + k4
                for vt in range(2):
                    x = xscr[t, NB * k:NB * k + NB, 128 * vt:128 * vt + 128]
                    xs[vt][k4] = pltpu.roll(x, PITCH * k4, 1) if k4 else x
            for v in range(NV):
                vt, s = VSLOT[v]
                rel = (lane - NB * s + 128) % 128 // PITCH
                yv = xs[vt][3]
                for k4 in range(3):
                    yv = jnp.where(rel == k4, xs[vt][k4], yv)
                if s:
                    yv = pltpu.roll(yv, 128 - NB * s, 1)
                ybuf[NB * v:NB * v + NB, 128 * h:128 * h + 128] = yv
        zz = jnp.dot(ybuf[...].astype(bf16), bd[...], preferred_element_type=f32)
        for h in range(2):
            b = 2 * g + h
            ek = jnp.zeros((NB, 128), f32)
            for k4 in range(4):
                ek = jnp.where(lane // PITCH == k4, ekt[PITCH * k4:PITCH * k4 + NB, b:b + 1], ek)
            diff = eps[h] - ek
            occ = jax.nn.sigmoid(ek * (-1.0 / KT)) - jax.nn.sigmoid(eps[h] * (-1.0 / KT))
            acc = jnp.zeros((NB, 128), f32)
            for v in range(NV):
                zv = zz[NB * v:NB * v + NB, 128 * h:128 * h + 128]
                d = diff - freq_ref[q, NV * vq + v]
                st = zv * zv * jnp.exp(d * d * (-1.0 / (2 * SIGMA * SIGMA)))
                acc = acc + st
                so = st * occ
                phacc[v] += so[0:8] + so[8:16] + so[16:24]
            aes[NB * g:NB * g + NB, 128 * h:128 * h + 128] = acc
    r3 = lax.broadcasted_iota(jnp.int32, (256, 128), 0)
    c3 = lax.broadcasted_iota(jnp.int32, (256, 128), 1)
    fold = jnp.where(c3 == (r3 // 128) * 64 + 4 * t + (r3 % 128) // PITCH, 1.0, 0.0).astype(f32)
    acc_ref[...] += jnp.dot(aes[...], fold, preferred_element_type=f32, precision=lax.Precision.HIGHEST)


def pack_sums(phacc, acc_ref, el_ref):
    f32 = jnp.float32
    lane = lax.broadcasted_iota(jnp.int32, (1, 128), 1)
    sums = jnp.concatenate([jnp.sum(phacc[v], axis=0, keepdims=True) for v in range(NV)]
                           + [jnp.zeros((16 - NV, 128), f32)], axis=0)
    sums = jnp.sum(sums, axis=1, keepdims=True)
    phonon = jnp.where(lane == 96, sums[0:8], 0.0) + jnp.where(lane == 97, sums[8:16], 0.0)
    for b in range(16):
        out = phonon
        for u in range(3):
            a = NB * (b // 2) + 8 * u
            piece = jnp.where(lane // 64 == b % 2, acc_ref[a:a + 8, :], 0.0)
            shift = (32 * u + 64 * (b % 2)) % 128
            out = out + (pltpu.roll(piece, shift, 1) if shift else piece)
        el_ref[b] = out


def rotate(coup_ref, rot_ref, sp, us, rs_ref):
    f32, bf16 = jnp.float32, jnp.bfloat16
    row = lax.broadcasted_iota(jnp.int32, (128, 1), 0)
    v = row % NM
    s = v % NV
    far = jnp.where(s >= 5, 1, 0)
    column = 256 * (v // NV) + 128 * far + NB * (s - 5 * far) + row // NM
    column = jnp.where(row < 3 * NM, column, -1024)
    lanes = lax.broadcasted_iota(jnp.int32, (128, 1024), 1)
    for g in range(8):
        sp[128 * g:128 * g + 128, :] = jnp.where(lanes == column + 3 * g, 1.0, 0.0).astype(bf16)
    rot = rot_ref[...].astype(f32)
    for q in range(4):
        rq = jnp.concatenate([rot[:, q, :], jnp.zeros((NM, 128 - NM), f32)], axis=1)
        rp = [(pltpu.roll(rq, NM * a, 1) if a else rq).astype(bf16) for a in range(3)]
        for r in range(2):
            ct = jnp.transpose(coup_ref[q, r].astype(f32))
            u = jnp.zeros((8 * NB, 128), f32)
            for a in range(3):
                rows = jnp.concatenate([ct[NB * (3 * g + a):NB * (3 * g + a) + NB] for g in range(8)], axis=0)
                u = u + jnp.dot(rows.astype(bf16), rp[a], preferred_element_type=f32)
            for g in range(8):
                us[NB * (2 * q + r):NB * (2 * q + r) + NB, 128 * g:128 * g + 128] = u[NB * g:NB * g + NB]
    out = jnp.dot(us[...].astype(bf16), sp[...], preferred_element_type=f32).astype(bf16)
    for q in range(4):
        for b in range(4):
            rs_ref[q, b] = out[48 * q:48 * q + 48, 256 * b:256 * b + 256]


def place():
    ka, pb, row = lax.axis_index("ka"), lax.axis_index("pb"), lax.axis_index("row")
    return ka // 2, ka % 2, row, pb // 8, pb % 8


def device(y, core, x, y_lo, z):
    return {"ka": 2 * y + core, "pb": 8 * y_lo + z, "row": x}


def phases(c, kp_ref, lat_ref, widen, pscr):
    f32 = jnp.float32
    lat = jnp.transpose(jnp.concatenate([lat_ref[...].astype(f32), jnp.zeros((5, NR), f32)], axis=0))
    for u in range(4):
        cols = pl.ds(pl.multiple_of(256 * u + 128 * c, 128), 128)
        arg = (lat[:, 0:1] * kp_ref[0:1, cols] + lat[:, 1:2] * kp_ref[1:2, cols]
               + lat[:, 2:3] * kp_ref[2:3, cols])
        ph = jnp.cos(2.0 * math.pi * arg).astype(jnp.bfloat16)
        pscr[128 * u:128 * u + 128, :] = lax.dot_general(
            ph, widen, (((0,), (0,)), ((), ())), preferred_element_type=f32)


def mega_kernel(kq_ref, freq_ref, kp_ref, lat_ref, coup_ref, rot_ref, eg_ref, et_ref,
                electron_ref, phonon_ref, sp, us, rs_ref, rt, eig, etab, pscr, etscr, wa, wb, xscr, bds, ybufs, aes, phacc, acc_ref,
                el, got, mine, peers, half,
                own, r_send, r_recv, t_send, t_recv, e_send, e_recv,
                up_send, up_recv, dn_send, dn_recv, ut_send, ut_recv, dt_send, dt_recv,
                rf_send, rf_recv, ef_send, ef_recv, tf_send, tf_recv,
                a_send, a_recv, b_send, b_recv, p_send, p_recv):
    f32 = jnp.float32
    y, c, x, w, z = place()
    me = y * 4 + x
    partner = device(y, 1 - c, x, w, z)
    above = device(y, c, x, w, (z + 1) % 8)
    below = device(y, c, x, w, (z + 7) % 8)
    plane, column = [], []
    for d in range(1, 16):
        yy, xx = (y + d // 4) % 4, (x + d % 4) % 4
        plane.append((yy, xx, device(yy, c, xx, w, z)))
        ww, zz = (w + d // 8) % 2, (z + d % 8) % 8
        column.append(device(y, c, x, ww, zz))

    barrier = pltpu.get_barrier_semaphore()
    for target in [o[2] for o in plane] + column + [partner]:
        pl.semaphore_signal(barrier, inc=1, device_id=target, device_id_type=pl.DeviceIdType.MESH)

    local = [
        pltpu.make_async_copy(eg_ref.at[z], eig.at[32 * z + 16 * c + me], own.at[0]),
        pltpu.make_async_copy(et_ref.at[pl.ds(z, 1)], etab.at[pl.ds(32 * z + 16 * c + me, 1)], own.at[1]),
    ]
    for cp in local:
        cp.start()
    rotate(coup_ref, rot_ref, sp, us, rs_ref)
    pl.semaphore_wait(barrier, 31)

    copies = []

    def send(src, dst, s, r, target):
        cp = pltpu.make_async_remote_copy(src_ref=src, dst_ref=dst, send_sem=s, recv_sem=r, device_id=target,
                                          device_id_type=pl.DeviceIdType.MESH)
        cp.start()
        return cp

    def arrival(ref, recv):
        pltpu.make_async_copy(ref, ref, recv).wait()

    def tiles(t, core):
        return eig.at[pl.ds(32 * t + 16 * core, 16)]

    def rows(t, core):
        return etab.at[pl.ds(pl.multiple_of(32 * t + 16 * core, 16), 16)]

    here = 32 * z + 16 * c + me
    for n, (yy, xx, target) in enumerate(plane):
        copies.append(send(eg_ref.at[z], eig.at[here], e_send.at[n], e_recv.at[n], target))
        copies.append(send(et_ref.at[pl.ds(z, 1)], etab.at[pl.ds(here, 1)], t_send.at[n], t_recv.at[n], target))
    for n, (yy, xx, target) in enumerate(plane):
        copies.append(send(rs_ref.at[yy, xx], rt.at[y, c, x], r_send.at[n], r_recv.at[n], target))

    local.append(pltpu.make_async_copy(rs_ref.at[y, x], rt.at[y, c, x], own.at[2]))
    local[2].start()
    spread, widen = constants()
    phases(c, kp_ref, lat_ref, widen, pscr)
    bds[...] = jnp.zeros_like(bds)
    phacc[...] = jnp.zeros_like(phacc)
    acc_ref[...] = jnp.zeros_like(acc_ref)

    def ring(step):
        up, dn = (z + 8 - step) % 8, (z + step) % 8
        if step:
            arrival(tiles(up, c), up_recv.at[step - 1])
            arrival(rows(up, c), ut_recv.at[step - 1])
        if step < 4:
            send(tiles(up, c), tiles(up, c), up_send.at[step], up_recv.at[step], above)
            send(rows(up, c), rows(up, c), ut_send.at[step], ut_recv.at[step], above)
        if 0 < step < 4:
            arrival(tiles(dn, c), dn_recv.at[step - 1])
            arrival(rows(dn, c), dt_recv.at[step - 1])
        if step < 3:
            send(tiles(dn, c), tiles(dn, c), dn_send.at[step], dn_recv.at[step], below)
            send(rows(dn, c), rows(dn, c), dt_send.at[step], dt_recv.at[step], below)
        for f, t in [(step, up)] + ([(4 + step, dn)] if 0 < step < 4 else []):
            send(tiles(t, c), tiles(t, c), ef_send.at[f], ef_recv.at[f], partner)
            send(rows(t, c), rows(t, c), tf_send.at[f], tf_recv.at[f], partner)

    def slice_of(f):
        return (z + 8 - f) % 8 if f < 5 else (z + f - 4) % 8

    for cp in local:
        cp.wait()
    for n in range(15):
        d = n + 1
        b = (y + 4 - d // 4) % 4 * 4 + (x + 4 - d % 4) % 4
        arrival(eig.at[32 * z + 16 * c + b], e_recv.at[n])
        arrival(etab.at[pl.ds(32 * z + 16 * c + b, 1)], t_recv.at[n])
    ring(0)
    ring(1)
    for dy in range(4):
        yy = (y + 4 - dy) % 4
        for dx in range(4):
            if dy or dx:
                arrival(rt.at[yy, c, (x + 4 - dx) % 4], r_recv.at[4 * dy + dx - 1])
        copies.append(send(rt.at[yy, c], rt.at[yy, c], rf_send.at[dy], rf_recv.at[dy], partner))
    for dy in range(4):
        arrival(rt.at[(y + 4 - dy) % 4, 1 - c], rf_recv.at[dy])

    def right(i, _):
        for step, at in ((2, 1), (3, 3), (4, 5)):
            pl.when(i == at)(lambda step=step: ring(step))
        t = (z + 8 + (1 - 2 * (i % 2)) * ((i + 1) // 2)) % 8
        right_stage(t, c, rt, eig, spread, pscr, etscr, (wa, wb), xscr)
        return 0
    lax.fori_loop(0, 8, right, 0)

    for f in range(8):
        arrival(tiles(slice_of(f), 1 - c), ef_recv.at[f])
        arrival(rows(slice_of(f), 1 - c), tf_recv.at[f])

    def final(t, _):
        final_stage(t, c, y, x, kq_ref, freq_ref, eig, etab, xscr, bds, ybufs, aes, phacc, acc_ref)
        return 0
    lax.fori_loop(0, 8, final, 0)
    pack_sums(phacc, acc_ref, el)

    for n, (yy, xx, target) in enumerate(plane):
        copies.append(send(el.at[yy * 4 + xx], got.at[me], a_send.at[n], a_recv.at[n], target))
    for n in range(15):
        d = n + 1
        arrival(got.at[(y + 4 - d // 4) % 4 * 4 + (x + 4 - d % 4) % 4], a_recv.at[n])
    lane = lax.broadcasted_iota(jnp.int32, (8, 128), 1)
    total = jnp.zeros((8, 128), f32)
    phonon = jnp.zeros((8, 128), f32)
    for s in range(16):
        tile = jnp.where(me == s, el[s], got[s])
        total = total + tile
        phonon = phonon + pltpu.roll(jnp.where((lane == 96) | (lane == 97), tile, 0.0), (2 * s + 32) % 128, 1)
    mine[...] = total
    half[0] = phonon
    for n, target in enumerate(column):
        copies.append(send(mine, peers.at[w * 8 + z], b_send.at[n], b_recv.at[n], target))
    copies.append(send(half.at[0], half.at[1], p_send.at[0], p_recv.at[0], partner))
    for n in range(15):
        d = n + 1
        arrival(peers.at[(w + 2 - d // 8) % 2 * 8 + (z + 8 - d % 8) % 8], b_recv.at[n])
    arrival(half.at[1], p_recv.at[0])
    acc = jnp.zeros((8, 128), f32)
    for s in range(16):
        acc = acc + jnp.where(w * 8 + z == s, total, peers[s])
    norm = 1.0 / (math.sqrt(2.0 * math.pi) * SIGMA)
    acc = jnp.concatenate([acc, pltpu.roll(acc, 96, 1), pltpu.roll(acc, 64, 1)], axis=0)
    electron_ref[...] = acc[:, 0:32] * (norm / 55296.0)
    both = half[0] + half[1]
    owner = lax.broadcasted_iota(jnp.int32, (8, 128), 0)
    spot = lax.broadcasted_iota(jnp.int32, (128, 128), 0)
    mode = lax.broadcasted_iota(jnp.int32, (128, 128), 1)
    result = jnp.zeros((8, 128), f32)
    for s in range(8 if NV > 8 else NV):
        line = jnp.where(lane // 8 == owner, both[s:s + 1], 0.0)
        inner = 8 * (spot % 2) + s
        to = jnp.where((inner < NV) & (mode == NV * (spot // 2 % 4) + inner), 1.0, 0.0).astype(f32)
        result = result + jnp.dot(line, to, preferred_element_type=f32, precision=lax.Precision.HIGHEST)
    phonon_ref[...] = result[0:4, 0:NM] * (norm / 24576.0)

    for cp in copies:
        cp.wait_send()
    for step in range(4):
        arrival(tiles(z, c), up_send.at[step])
        arrival(rows(z, c), ut_send.at[step])
        if step < 3:
            arrival(tiles(z, c), dn_send.at[step])
            arrival(rows(z, c), dt_send.at[step])
    for f in range(8):
        arrival(tiles(z, c), ef_send.at[f])
        arrival(rows(z, c), tf_send.at[f])


def mega(kq, freq, kp, lat, coup, rot, eg, et):
    f32, bf16 = jnp.float32, jnp.bfloat16
    smem = pl.BlockSpec(memory_space=pltpu.SMEM)
    vmem = pl.BlockSpec(memory_space=pltpu.VMEM)
    dma = pltpu.SemaphoreType.DMA
    return pl.pallas_call(
        mega_kernel,
        out_shape=(jax.ShapeDtypeStruct((NB, 32), f32), jax.ShapeDtypeStruct((4, NM), f32)),
        in_specs=[smem, smem] + [vmem] * 6,
        out_specs=(vmem, vmem),
        scratch_shapes=[
            pltpu.VMEM((1024, 1024), bf16), pltpu.VMEM((192, 1024), f32), pltpu.VMEM((4, 4, 48, 256), bf16),
            pltpu.VMEM((4, 2, 4, 48, 256), bf16), pltpu.VMEM((256, NB, 128), bf16), pltpu.VMEM((256, 128), f32),
            pltpu.VMEM((512, NR * NB), f32), pltpu.VMEM((2048, 384), f32),
            pltpu.VMEM((384, NR * NB), bf16), pltpu.VMEM((384, NR * NB), bf16), pltpu.VMEM((8, 1536, 256), f32),
            pltpu.VMEM((4, 256, 256), bf16), pltpu.VMEM((4, NV * NB, 256), f32), pltpu.VMEM((8 * NB, 256), f32),
            pltpu.VMEM((NV, 8, 128), f32), pltpu.VMEM((8 * NB, 128), f32),
            pltpu.VMEM((16, 8, 128), f32), pltpu.VMEM((16, 8, 128), f32), pltpu.VMEM((8, 128), f32),
            pltpu.VMEM((16, 8, 128), f32), pltpu.VMEM((2, 8, 128), f32),
            dma((3,)), dma((15,)), dma((15,)), dma((15,)), dma((15,)), dma((15,)), dma((15,)),
            dma((4,)), dma((4,)), dma((3,)), dma((3,)), dma((4,)), dma((4,)), dma((3,)), dma((3,)),
            dma((4,)), dma((4,)), dma((8,)), dma((8,)), dma((8,)), dma((8,)),
            dma((15,)), dma((15,)), dma((15,)), dma((15,)), dma((1,)), dma((1,))],
        compiler_params=pltpu.CompilerParams(collective_id=0, has_side_effects=True, vmem_limit_bytes=60 << 20),
        name="linewidths",
    )(kq, freq, kp, lat, coup, rot, eg, et)


def on_device(coupling, rotation, freq, eigvec, energies, window, kq_index, kpoints, lattice):
    f32, bf16 = jnp.float32, jnp.bfloat16
    inside = jnp.arange(NB)[None, None, :] < window[:, None, None]
    eg = jnp.pad(jnp.where(inside, eigvec, jnp.zeros((), bf16)).reshape(8, 4, NB, NB), ((0, 0), (0, 0), (0, 0), (0, 8)))
    eg = eg.transpose(0, 2, 1, 3).reshape(8, NB, 128)
    et = jnp.pad(energies, ((0, 0), (0, 8))).reshape(8, 128)
    electron, phonon = mega(kq_index, freq, kpoints.T, lattice.T, coupling.reshape(4, 2, NM, NB * NB),
                            rotation.transpose(1, 0, 2), eg, et)
    return electron.T, phonon


def solution(mesh):
    return jax.shard_map(
        on_device,
        mesh=mesh,
        in_specs=(
            P("pb", ("ka", "row"), None),
            P("pb", None, None),
            P("pb", None),
            P(("ka", "row"), None, None),
            P(("ka", "row"), None),
            P(("ka", "row")),
            P("pb", None),
            P(),
            P(),
        ),
        out_specs=(P(("ka", "row"), None), P("pb", None)),
        check_vma=False,
    )
```

```python
import math

import jax
import jax.numpy as jnp
from jax import lax
from jax.experimental import pallas as pl
from jax.experimental.pallas import tpu as pltpu
from jax.sharding import PartitionSpec as P

SIGMA = 0.1
KT = 0.2
NB, NM, NR = 24, 36, 64
NV = 9
SHARP = math.sqrt(1.0 / (2.0 * SIGMA * SIGMA * math.log(2.0)))
PITCH = 32
VSLOT = [(v // 5, v % 5) for v in range(NV)]


def constants():
    f32, bf16 = jnp.float32, jnp.bfloat16
    r1 = lax.broadcasted_iota(jnp.int32, (NB, 384), 0)
    c1 = lax.broadcasted_iota(jnp.int32, (NB, 384), 1)
    spread = jnp.where(c1 % NB == r1, 1.0, 0.0).astype(bf16)
    r2 = lax.broadcasted_iota(jnp.int32, (NR, NR * NB), 0)
    c2 = lax.broadcasted_iota(jnp.int32, (NR, NR * NB), 1)
    widen = jnp.where(c2 // NB == r2, 1.0, 0.0).astype(bf16)
    return spread, widen


def right_steps(i, t, c, rt_ref, eig_ref, spread, pscr, etscr, wbufs, xscr):
    f32, bf16 = jnp.float32, jnp.bfloat16
    tt = jnp.concatenate([eig_ref[32 * t + 16 * c + b] for b in range(16)], axis=1)
    etscr[...] = lax.dot_general(tt, spread, (((0,), (0,)), ((), ())), preferred_element_type=f32)
    for sub in range(4):
        wbuf = wbufs[sub % 2]
        for pair in range(8):
            parts = []
            for kk in range(2):
                k = 16 * sub + 2 * pair + kk
                ek = etscr[PITCH * k:PITCH * k + NB, :]
                p = pscr[pl.ds((k // 4) * 32 + 4 * t + k % 4, 1), :]
                parts.append(jnp.concatenate([ek * p[:, 384 * a:384 * a + 384] for a in range(4)], axis=1))
            wbuf[48 * pair:48 * pair + 48, :] = jnp.concatenate(parts, axis=0).astype(bf16)
        xscr[i, 384 * sub:384 * sub + 384, :] = jnp.dot(wbuf[...], rt_ref[...].reshape(NR * NB, 256), preferred_element_type=f32)
        yield


def final_steps(i, t, c, q, vq, kq_ref, freq_ref, eig_ref, etab_ref, xscr, bds, ybufs, aes, phacc, acc_ref):
    f32, bf16 = jnp.float32, jnp.bfloat16
    lane = lax.broadcasted_iota(jnp.int32, (1, 128), 1)
    freqs = [freq_ref[q, NV * vq + v] * SHARP for v in range(NV)]
    ekt = jnp.transpose(etab_ref[pl.ds(pl.multiple_of(32 * t + 16 * c, 16), 16), :])
    sums = [jnp.zeros((8, 128), f32) for _ in range(NV)]
    for g in range(8):
        bd, ybuf = bds.at[g % 4], ybufs.at[g % 4]
        eps = []
        for h in range(2):
            b = 2 * g + h
            evec = jnp.zeros((1, 128), f32)
            for k4 in range(4):
                p = kq_ref[q, 4 * t + c * 128 + (b // 4) * 256 + (b % 4) * 32 + k4]
                tile = ((p >> 2) & 7) * 32 + ((p >> 7) & 1) * 16 + ((p >> 8) << 2) + ((p >> 5) & 3)
                sh = ((k4 - p) & 3) * PITCH
                here = lane // PITCH == k4
                e = pltpu.roll(eig_ref[tile].astype(f32), sh, 1)
                e = jnp.where(here, e, 0.0)
                e = jnp.concatenate([e, jnp.zeros((8, 128), f32)], axis=0).astype(bf16)
                bd[128 * h + PITCH * k4:128 * h + PITCH * k4 + PITCH, 128 * h:128 * h + 128] = e
                er = pltpu.roll(etab_ref[pl.ds(tile, 1), :], sh, 1)
                evec = jnp.where(here, er, evec)
            eps.append(evec)
        for h in range(2):
            xs = [[None] * 4 for _ in range(2)]
            for k4 in range(4):
                k = 8 * g + 4 * h + k4
                for vt in range(2):
                    x = xscr[i, NB * k:NB * k + NB, 128 * vt:128 * vt + 128]
                    xs[vt][k4] = pltpu.roll(x, PITCH * k4, 1) if k4 else x
            for v in range(NV):
                vt, s = VSLOT[v]
                rel = (lane - NB * s + 128) % 128 // PITCH
                yv = xs[vt][3]
                for k4 in range(3):
                    yv = jnp.where(rel == k4, xs[vt][k4], yv)
                if s:
                    yv = pltpu.roll(yv, 128 - NB * s, 1)
                ybuf[NB * v:NB * v + NB, 128 * h:128 * h + 128] = yv
        zz = jnp.dot(ybuf[...].astype(bf16), bd[...], preferred_element_type=f32)
        for h in range(2):
            b = 2 * g + h
            ek = jnp.zeros((NB, 128), f32)
            for k4 in range(4):
                ek = jnp.where(lane // PITCH == k4, ekt[PITCH * k4:PITCH * k4 + NB, b:b + 1], ek)
            diff = (eps[h] - ek) * SHARP
            occ = jax.nn.sigmoid(ek * (-1.0 / KT)) - jax.nn.sigmoid(eps[h] * (-1.0 / KT))
            acc = jnp.zeros((NB, 128), f32)
            for v in range(NV):
                zv = zz[NB * v:NB * v + NB, 128 * h:128 * h + 128]
                d = diff - freqs[v]
                st = zv * zv * jnp.exp2(-(d * d))
                acc = acc + st
                so = st * occ
                sums[v] = sums[v] + (so[0:8] + so[8:16] + so[16:24])
            aes[NB * g:NB * g + NB, 128 * h:128 * h + 128] = acc
        yield
    for v in range(NV):
        phacc[v] += sums[v]
    r3 = lax.broadcasted_iota(jnp.int32, (256, 128), 0)
    c3 = lax.broadcasted_iota(jnp.int32, (256, 128), 1)
    fold = jnp.where(c3 == (r3 // 128) * 64 + 4 * t + (r3 % 128) // PITCH, 1.0, 0.0).astype(f32)
    acc_ref[...] += jnp.dot(aes[...], fold, preferred_element_type=f32, precision=lax.Precision.HIGHEST)


def pack_sums(phacc, acc_ref, el_ref):
    f32 = jnp.float32
    lane = lax.broadcasted_iota(jnp.int32, (1, 128), 1)
    sums = jnp.concatenate([jnp.sum(phacc[v], axis=0, keepdims=True) for v in range(NV)]
                           + [jnp.zeros((16 - NV, 128), f32)], axis=0)
    sums = jnp.sum(sums, axis=1, keepdims=True)
    phonon = jnp.where(lane == 96, sums[0:8], 0.0) + jnp.where(lane == 97, sums[8:16], 0.0)
    for b in range(16):
        out = phonon
        for u in range(3):
            a = NB * (b // 2) + 8 * u
            piece = jnp.where(lane // 64 == b % 2, acc_ref[a:a + 8, :], 0.0)
            shift = (32 * u + 64 * (b % 2)) % 128
            out = out + (pltpu.roll(piece, shift, 1) if shift else piece)
        el_ref[4 * (b % 4) + b // 4] = out


def run(*steps):
    steps = list(steps)
    while steps:
        for s in list(steps):
            if next(s, "end") == "end":
                steps.remove(s)


def rotate(coup_ref, rot_ref, sp, us, rs_ref):
    f32, bf16 = jnp.float32, jnp.bfloat16
    row = lax.broadcasted_iota(jnp.int32, (128, 1), 0)
    v = row % NM
    s = v % NV
    far = jnp.where(s >= 5, 1, 0)
    column = 256 * (v // NV) + 128 * far + NB * (s - 5 * far) + row // NM
    column = jnp.where(row < 3 * NM, column, -1024)
    lanes = lax.broadcasted_iota(jnp.int32, (128, 1024), 1)
    for g in range(8):
        sp[128 * g:128 * g + 128, :] = jnp.where(lanes == column + 3 * g, 1.0, 0.0).astype(bf16)
    rot = rot_ref[...].astype(f32)
    for q in range(4):
        rq = jnp.concatenate([rot[:, q, :], jnp.zeros((NM, 128 - NM), f32)], axis=1)
        rp = [(pltpu.roll(rq, NM * a, 1) if a else rq).astype(bf16) for a in range(3)]
        for r in range(2):
            ct = jnp.transpose(coup_ref[q, r].astype(f32))
            u = jnp.zeros((8 * NB, 128), f32)
            for a in range(3):
                rows = jnp.concatenate([ct[NB * (3 * g + a):NB * (3 * g + a) + NB] for g in range(8)], axis=0)
                u = u + jnp.dot(rows.astype(bf16), rp[a], preferred_element_type=f32)
            for g in range(8):
                us[NB * (2 * q + r):NB * (2 * q + r) + NB, 128 * g:128 * g + 128] = u[NB * g:NB * g + NB]
    out = jnp.dot(us[...].astype(bf16), sp[...], preferred_element_type=f32).astype(bf16)
    for q in range(4):
        for b in range(4):
            rs_ref[q, b] = out[48 * q:48 * q + 48, 256 * b:256 * b + 256]


def own_slice(z, ev_ref, en_ref, win_ref):
    f32, bf16 = jnp.float32, jnp.bfloat16
    lane = lax.broadcasted_iota(jnp.int32, (1, 128), 1)
    pick = lax.broadcasted_iota(jnp.int32, (32, 128), 0) == 4 * z + lane // PITCH
    lim = jnp.dot(jnp.broadcast_to(win_ref[...], (8, 32)).astype(bf16), jnp.where(pick, 1.0, 0.0).astype(bf16),
                  preferred_element_type=f32)[0:1]
    band = lane % PITCH
    wide = jnp.dot(ev_ref[...], jnp.where(pick, 1.0, 0.0).astype(bf16), preferred_element_type=f32)
    row = lax.broadcasted_iota(jnp.int32, (NB * NB, 128), 0)
    keep = (row % NB == band) & (band.astype(f32) < lim)
    r4 = lax.broadcasted_iota(jnp.int32, (NB, NB * NB), 0)
    c4 = lax.broadcasted_iota(jnp.int32, (NB, NB * NB), 1)
    gather = jnp.where(c4 // NB == r4, 1.0, 0.0).astype(bf16)
    vectors = jnp.dot(gather, jnp.where(keep, wide, 0.0).astype(bf16), preferred_element_type=f32)
    levels = jnp.dot(en_ref[...], jnp.where(pick, 1.0, 0.0).astype(f32), preferred_element_type=f32,
                     precision=lax.Precision.HIGHEST)
    levels = jnp.where(lax.broadcasted_iota(jnp.int32, (NB, 128), 0) == band, levels, 0.0)
    return vectors.astype(bf16), jnp.sum(levels, axis=0, keepdims=True)


def place():
    ka, pb, row = lax.axis_index("ka"), lax.axis_index("pb"), lax.axis_index("row")
    return ka // 2, ka % 2, row, pb // 8, pb % 8


def device(y, core, x, y_lo, z):
    return {"ka": 2 * y + core, "pb": 8 * y_lo + z, "row": x}


def phases(c, kp_ref, lat_ref, widen, pscr):
    f32 = jnp.float32
    lat = jnp.transpose(jnp.concatenate([lat_ref[...].astype(f32), jnp.zeros((5, NR), f32)], axis=0))
    for u in range(4):
        cols = pl.ds(pl.multiple_of(256 * u + 128 * c, 128), 128)
        arg = (lat[:, 0:1] * kp_ref[0:1, cols] + lat[:, 1:2] * kp_ref[1:2, cols]
               + lat[:, 2:3] * kp_ref[2:3, cols])
        ph = jnp.cos(2.0 * math.pi * arg).astype(jnp.bfloat16)
        pscr[128 * u:128 * u + 128, :] = lax.dot_general(
            ph, widen, (((0,), (0,)), ((), ())), preferred_element_type=f32)


def mega_kernel(kq_ref, freq_ref, kp_ref, lat_ref, coup_ref, rot_ref, ev_ref, en_ref, win_ref,
                electron_ref, phonon_ref, sp, us, rs_ref, rt, eig, etab, pscr, etscr, wa, wb, xa, xb, bds, ybufs, aes, phacc, acc_ref,
                el, got, tiles2, got2, mine, peers, half,
                own, r_send, r_recv, t_send, t_recv, e_send, e_recv,
                up_send, up_recv, dn_send, dn_recv, ut_send, ut_recv, dt_send, dt_recv,
                rf_send, rf_recv, ef_send, ef_recv, tf_send, tf_recv,
                a_send, a_recv, b_send, b_recv, p_send, p_recv):
    f32 = jnp.float32
    y, c, x, w, z = place()
    me = y * 4 + x
    partner = device(y, 1 - c, x, w, z)
    above = device(y, c, x, w, (z + 1) % 8)
    below = device(y, c, x, w, (z + 7) % 8)
    plane, column = [], []
    for d in range(1, 16):
        yy, xx = (y + d // 4) % 4, (x + d % 4) % 4
        plane.append((yy, xx, device(yy, c, xx, w, z)))
        ww, zz = (w + d // 8) % 2, (z + d % 8) % 8
        column.append(device(y, c, x, ww, zz))

    barrier = pltpu.get_barrier_semaphore()
    for target in [o[2] for o in plane] + column + [partner]:
        pl.semaphore_signal(barrier, inc=1, device_id=target, device_id_type=pl.DeviceIdType.MESH)

    here = 32 * z + 16 * c + me
    eig[here], etab[pl.ds(here, 1), :] = own_slice(z, ev_ref, en_ref, win_ref)
    rotate(coup_ref, rot_ref, sp, us, rs_ref)
    pl.semaphore_wait(barrier, 31)

    copies = []

    def send(src, dst, s, r, target):
        cp = pltpu.make_async_remote_copy(src_ref=src, dst_ref=dst, send_sem=s, recv_sem=r, device_id=target,
                                          device_id_type=pl.DeviceIdType.MESH)
        cp.start()
        return cp

    def arrival(ref, recv):
        pltpu.make_async_copy(ref, ref, recv).wait()

    def tiles(t, core):
        return eig.at[pl.ds(32 * t + 16 * core, 16)]

    def rows(t, core):
        return etab.at[pl.ds(pl.multiple_of(32 * t + 16 * core, 16), 16)]

    for n, (yy, xx, target) in enumerate(plane):
        copies.append(send(eig.at[here], eig.at[here], e_send.at[n], e_recv.at[n], target))
        copies.append(send(etab.at[pl.ds(here, 1)], etab.at[pl.ds(here, 1)], t_send.at[n], t_recv.at[n], target))
    for n, (yy, xx, target) in enumerate(plane):
        copies.append(send(rs_ref.at[yy, xx], rt.at[y, c, x], r_send.at[n], r_recv.at[n], target))

    local = pltpu.make_async_copy(rs_ref.at[y, x], rt.at[y, c, x], own.at[0])
    local.start()
    spread, widen = constants()
    phases(c, kp_ref, lat_ref, widen, pscr)
    bds[...] = jnp.zeros_like(bds)
    phacc[...] = jnp.zeros_like(phacc)
    acc_ref[...] = jnp.zeros_like(acc_ref)

    def ring(step):
        up, dn = (z + 8 - step) % 8, (z + step) % 8
        if step:
            arrival(tiles(up, c), up_recv.at[step - 1])
            arrival(rows(up, c), ut_recv.at[step - 1])
        if step < 4:
            send(tiles(up, c), tiles(up, c), up_send.at[step], up_recv.at[step], above)
            send(rows(up, c), rows(up, c), ut_send.at[step], ut_recv.at[step], above)
        if 0 < step < 4:
            arrival(tiles(dn, c), dn_recv.at[step - 1])
            arrival(rows(dn, c), dt_recv.at[step - 1])
        if step < 3:
            send(tiles(dn, c), tiles(dn, c), dn_send.at[step], dn_recv.at[step], below)
            send(rows(dn, c), rows(dn, c), dt_send.at[step], dt_recv.at[step], below)
        for f, t in [(step, up)] + ([(4 + step, dn)] if 0 < step < 4 else []):
            send(tiles(t, c), tiles(t, c), ef_send.at[f], ef_recv.at[f], partner)
            send(rows(t, c), rows(t, c), tf_send.at[f], tf_recv.at[f], partner)

    def slice_of(f):
        return (z + 8 - f) % 8 if f < 5 else (z + f - 4) % 8

    local.wait()
    for n in range(15):
        d = n + 1
        b = (y + 4 - d // 4) % 4 * 4 + (x + 4 - d % 4) % 4
        arrival(eig.at[32 * z + 16 * c + b], e_recv.at[n])
        arrival(etab.at[pl.ds(32 * z + 16 * c + b, 1)], t_recv.at[n])
    ring(0)
    ring(1)
    for dy in range(4):
        yy = (y + 4 - dy) % 4
        for dx in range(4):
            if dy or dx:
                arrival(rt.at[yy, c, (x + 4 - dx) % 4], r_recv.at[4 * dy + dx - 1])
        copies.append(send(rt.at[yy, c], rt.at[yy, c], rf_send.at[dy], rf_recv.at[dy], partner))
    for dy in range(4):
        arrival(rt.at[(y + 4 - dy) % 4, 1 - c], rf_recv.at[dy])

    def slice_at(i):
        return (z + 8 + (1 - 2 * (i % 2)) * ((i + 1) // 2)) % 8

    rargs = (c, rt, eig, spread, pscr, etscr, (wa, wb))
    fargs = (c, y, x, kq_ref, freq_ref, eig, etab)
    sums = (bds, ybufs, aes, phacc, acc_ref)

    def first(i, _):
        for step in (2, 3, 4):
            pl.when(i == step - 2 + step // 4)(lambda step=step: ring(step))
        run(right_steps(i, slice_at(i), *rargs, xa))
        return 0
    lax.fori_loop(0, 4, first, 0)

    for f in range(8):
        arrival(tiles(slice_of(f), 1 - c), ef_recv.at[f])
        arrival(rows(slice_of(f), 1 - c), tf_recv.at[f])

    def both_stages(i, _):
        run(final_steps(i, slice_at(i), *fargs, xa, *sums), right_steps(i, slice_at(i + 4), *rargs, xb))
        return 0
    lax.fori_loop(0, 4, both_stages, 0)

    def last(i, _):
        run(final_steps(i, slice_at(i + 4), *fargs, xb, *sums))
        return 0
    lax.fori_loop(0, 4, last, 0)
    pack_sums(phacc, acc_ref, el)

    for d in range(1, 4):
        xx = (x + d) % 4
        copies.append(send(el.at[pl.ds(4 * xx, 4)], got.at[pl.ds(4 * x, 4)], a_send.at[d - 1], a_recv.at[d - 1],
                           device(y, c, xx, w, z)))
    for d in range(1, 4):
        arrival(got.at[pl.ds(4 * ((x + 4 - d) % 4), 4)], a_recv.at[d - 1])
    lane = lax.broadcasted_iota(jnp.int32, (8, 128), 1)
    for yy in range(4):
        total = jnp.zeros((8, 128), f32)
        for s in range(4):
            tile = jnp.where(x == s, el[4 * s + yy], got[4 * s + yy])
            total = total + jnp.where(lane < 96, tile, 0.0)
            phonon = jnp.where((lane == 96) | (lane == 97), tile, 0.0)
            total = total + (pltpu.roll(phonon, 2 * s, 1) if s else phonon)
        tiles2[yy] = total
    for d in range(1, 4):
        yy = (y + d) % 4
        copies.append(send(tiles2.at[yy], got2.at[y], a_send.at[d + 2], a_recv.at[d + 2], device(yy, c, x, w, z)))
    for d in range(1, 4):
        arrival(got2.at[(y + 4 - d) % 4], a_recv.at[d + 2])
    total = jnp.zeros((8, 128), f32)
    phonon = jnp.zeros((8, 128), f32)
    for s in range(4):
        tile = jnp.where(y == s, tiles2[s], got2[s])
        total = total + jnp.where(lane < 96, tile, 0.0)
        phonon = phonon + pltpu.roll(jnp.where((lane >= 96) & (lane < 104), tile, 0.0), 32 + 8 * s, 1)
    mine[...] = total
    half[0] = phonon
    for n, target in enumerate(column):
        copies.append(send(mine, peers.at[w * 8 + z], b_send.at[n], b_recv.at[n], target))
    copies.append(send(half.at[0], half.at[1], p_send.at[0], p_recv.at[0], partner))
    for n in range(15):
        d = n + 1
        arrival(peers.at[(w + 2 - d // 8) % 2 * 8 + (z + 8 - d % 8) % 8], b_recv.at[n])
    arrival(half.at[1], p_recv.at[0])
    acc = jnp.zeros((8, 128), f32)
    for s in range(16):
        acc = acc + jnp.where(w * 8 + z == s, total, peers[s])
    norm = 1.0 / (math.sqrt(2.0 * math.pi) * SIGMA)
    acc = jnp.concatenate([acc, pltpu.roll(acc, 96, 1), pltpu.roll(acc, 64, 1)], axis=0)
    electron_ref[...] = acc[:, 0:32] * (norm / 55296.0)
    both = half[0] + half[1]
    owner = lax.broadcasted_iota(jnp.int32, (8, 128), 0)
    spot = lax.broadcasted_iota(jnp.int32, (128, 128), 0)
    mode = lax.broadcasted_iota(jnp.int32, (128, 128), 1)
    result = jnp.zeros((8, 128), f32)
    for s in range(8 if NV > 8 else NV):
        line = jnp.where(lane // 8 == owner, both[s:s + 1], 0.0)
        inner = 8 * (spot % 2) + s
        to = jnp.where((inner < NV) & (mode == NV * (spot // 2 % 4) + inner), 1.0, 0.0).astype(f32)
        result = result + jnp.dot(line, to, preferred_element_type=f32, precision=lax.Precision.HIGHEST)
    phonon_ref[...] = result[0:4, 0:NM] * (norm / 24576.0)

    for cp in copies:
        cp.wait_send()
    for step in range(4):
        arrival(tiles(z, c), up_send.at[step])
        arrival(rows(z, c), ut_send.at[step])
        if step < 3:
            arrival(tiles(z, c), dn_send.at[step])
            arrival(rows(z, c), dt_send.at[step])
    for f in range(8):
        arrival(tiles(z, c), ef_send.at[f])
        arrival(rows(z, c), tf_send.at[f])


def mega(kq, freq, kp, lat, coup, rot, ev, en, win):
    f32, bf16 = jnp.float32, jnp.bfloat16
    smem = pl.BlockSpec(memory_space=pltpu.SMEM)
    vmem = pl.BlockSpec(memory_space=pltpu.VMEM)
    dma = pltpu.SemaphoreType.DMA
    return pl.pallas_call(
        mega_kernel,
        out_shape=(jax.ShapeDtypeStruct((NB, 32), f32), jax.ShapeDtypeStruct((4, NM), f32)),
        in_specs=[smem, smem] + [vmem] * 7,
        out_specs=(vmem, vmem),
        scratch_shapes=[
            pltpu.VMEM((1024, 1024), bf16), pltpu.VMEM((192, 1024), f32), pltpu.VMEM((4, 4, 48, 256), bf16),
            pltpu.VMEM((4, 2, 4, 48, 256), bf16), pltpu.VMEM((256, NB, 128), bf16), pltpu.VMEM((256, 128), f32),
            pltpu.VMEM((512, NR * NB), f32), pltpu.VMEM((2048, 384), f32),
            pltpu.VMEM((384, NR * NB), bf16), pltpu.VMEM((384, NR * NB), bf16), pltpu.VMEM((4, 1536, 256), f32), pltpu.VMEM((4, 1536, 256), f32),
            pltpu.VMEM((4, 256, 256), bf16), pltpu.VMEM((4, NV * NB, 256), f32), pltpu.VMEM((8 * NB, 256), f32),
            pltpu.VMEM((NV, 8, 128), f32), pltpu.VMEM((8 * NB, 128), f32),
            pltpu.VMEM((16, 8, 128), f32), pltpu.VMEM((16, 8, 128), f32), pltpu.VMEM((4, 8, 128), f32),
            pltpu.VMEM((4, 8, 128), f32), pltpu.VMEM((8, 128), f32),
            pltpu.VMEM((16, 8, 128), f32), pltpu.VMEM((2, 8, 128), f32),
            dma((1,)), dma((15,)), dma((15,)), dma((15,)), dma((15,)), dma((15,)), dma((15,)),
            dma((4,)), dma((4,)), dma((3,)), dma((3,)), dma((4,)), dma((4,)), dma((3,)), dma((3,)),
            dma((4,)), dma((4,)), dma((8,)), dma((8,)), dma((8,)), dma((8,)),
            dma((6,)), dma((6,)), dma((15,)), dma((15,)), dma((1,)), dma((1,))],
        compiler_params=pltpu.CompilerParams(collective_id=0, has_side_effects=True, vmem_limit_bytes=60 << 20),
        name="linewidths",
    )(kq, freq, kp, lat, coup, rot, ev, en, win)


def on_device(coupling, rotation, freq, eigvec, energies, window, kq_index, kpoints, lattice):
    electron, phonon = mega(kq_index, freq, kpoints.T, lattice.T, coupling.reshape(4, 2, NM, NB * NB),
                            rotation.transpose(1, 0, 2), eigvec.transpose(1, 2, 0).reshape(NB * NB, 32), energies.T,
                            window.reshape(1, 32))
    return electron.T, phonon


def solution(mesh):
    return jax.shard_map(
        on_device,
        mesh=mesh,
        in_specs=(
            P("pb", ("ka", "row"), None),
            P("pb", None, None),
            P("pb", None),
            P(("ka", "row"), None, None),
            P(("ka", "row"), None),
            P(("ka", "row")),
            P("pb", None),
            P(),
            P(),
        ),
        out_specs=(P(("ka", "row"), None), P("pb", None)),
        check_vma=False,
    )
```

```python
import math

import jax
import jax.numpy as jnp
from jax import lax
from jax.experimental import pallas as pl
from jax.experimental.pallas import tpu as pltpu
from jax.sharding import PartitionSpec as P

SIGMA = 0.1
KT = 0.2
NB, NM, NR = 24, 36, 64
NV = 9
SHARP = math.sqrt(1.0 / (2.0 * SIGMA * SIGMA * math.log(2.0)))
PITCH = 32
VSLOT = [(v // 5, v % 5) for v in range(NV)]


def constants():
    f32, bf16 = jnp.float32, jnp.bfloat16
    r1 = lax.broadcasted_iota(jnp.int32, (NB, 384), 0)
    c1 = lax.broadcasted_iota(jnp.int32, (NB, 384), 1)
    spread = jnp.where(c1 % NB == r1, 1.0, 0.0).astype(bf16)
    r2 = lax.broadcasted_iota(jnp.int32, (NR, NR * NB), 0)
    c2 = lax.broadcasted_iota(jnp.int32, (NR, NR * NB), 1)
    widen = jnp.where(c2 // NB == r2, 1.0, 0.0).astype(bf16)
    return spread, widen


def right_steps(i, t, c, rt_ref, eig_ref, spread, pscr, etscr, wbufs, xscr):
    f32, bf16 = jnp.float32, jnp.bfloat16
    tt = jnp.concatenate([eig_ref[32 * t + 16 * c + b] for b in range(16)], axis=1)
    etscr[...] = lax.dot_general(tt, spread, (((0,), (0,)), ((), ())), preferred_element_type=f32)
    for sub in range(4):
        wbuf = wbufs[sub % 2]
        for pair in range(8):
            parts = []
            for kk in range(2):
                k = 16 * sub + 2 * pair + kk
                ek = etscr[PITCH * k:PITCH * k + NB, :]
                p = pscr[pl.ds((k // 4) * 32 + 4 * t + k % 4, 1), :]
                parts.append(jnp.concatenate([ek * p[:, 384 * a:384 * a + 384] for a in range(4)], axis=1))
            wbuf[48 * pair:48 * pair + 48, :] = jnp.concatenate(parts, axis=0).astype(bf16)
        xscr[i, 384 * sub:384 * sub + 384, :] = jnp.dot(wbuf[...], rt_ref[...].reshape(NR * NB, 256), preferred_element_type=f32)
        yield


def final_steps(i, t, c, q, vq, kq_ref, freq_ref, eig_ref, etab_ref, xscr, bds, ybufs, aes, phacc, acc_ref):
    f32, bf16 = jnp.float32, jnp.bfloat16
    lane = lax.broadcasted_iota(jnp.int32, (1, 128), 1)
    freqs = [freq_ref[q, NV * vq + v] * SHARP for v in range(NV)]
    ekt = jnp.transpose(etab_ref[pl.ds(pl.multiple_of(32 * t + 16 * c, 16), 16), :])
    sums = [jnp.zeros((8, 128), f32) for _ in range(NV)]
    for g in range(8):
        bd, ybuf = bds.at[g % 4], ybufs.at[g % 4]
        eps = []
        for h in range(2):
            b = 2 * g + h
            evec = jnp.zeros((1, 128), f32)
            for k4 in range(4):
                p = kq_ref[q, 4 * t + c * 128 + (b // 4) * 256 + (b % 4) * 32 + k4]
                tile = ((p >> 2) & 7) * 32 + ((p >> 7) & 1) * 16 + ((p >> 8) << 2) + ((p >> 5) & 3)
                sh = ((k4 - p) & 3) * PITCH
                here = lane // PITCH == k4
                e = pltpu.roll(eig_ref[tile].astype(f32), sh, 1)
                e = jnp.where(here, e, 0.0)
                e = jnp.concatenate([e, jnp.zeros((8, 128), f32)], axis=0).astype(bf16)
                bd[128 * h + PITCH * k4:128 * h + PITCH * k4 + PITCH, 128 * h:128 * h + 128] = e
                er = pltpu.roll(etab_ref[pl.ds(tile, 1), :], sh, 1)
                evec = jnp.where(here, er, evec)
            eps.append(evec)
        for h in range(2):
            xs = [[None] * 4 for _ in range(2)]
            for k4 in range(4):
                k = 8 * g + 4 * h + k4
                for vt in range(2):
                    x = xscr[i, NB * k:NB * k + NB, 128 * vt:128 * vt + 128]
                    xs[vt][k4] = pltpu.roll(x, PITCH * k4, 1) if k4 else x
            for v in range(NV):
                vt, s = VSLOT[v]
                rel = (lane - NB * s + 128) % 128 // PITCH
                yv = xs[vt][3]
                for k4 in range(3):
                    yv = jnp.where(rel == k4, xs[vt][k4], yv)
                if s:
                    yv = pltpu.roll(yv, 128 - NB * s, 1)
                ybuf[NB * v:NB * v + NB, 128 * h:128 * h + 128] = yv
        zz = jnp.dot(ybuf[...].astype(bf16), bd[...], preferred_element_type=f32)
        for h in range(2):
            b = 2 * g + h
            ek = jnp.zeros((NB, 128), f32)
            for k4 in range(4):
                ek = jnp.where(lane // PITCH == k4, ekt[PITCH * k4:PITCH * k4 + NB, b:b + 1], ek)
            diff = (eps[h] - ek) * SHARP
            occ = jax.nn.sigmoid(ek * (-1.0 / KT)) - jax.nn.sigmoid(eps[h] * (-1.0 / KT))
            acc = jnp.zeros((NB, 128), f32)
            for v in range(NV):
                zv = zz[NB * v:NB * v + NB, 128 * h:128 * h + 128]
                d = diff - freqs[v]
                st = zv * zv * jnp.exp2(-(d * d))
                acc = acc + st
                so = st * occ
                sums[v] = sums[v] + (so[0:8] + so[8:16] + so[16:24])
            aes[NB * g:NB * g + NB, 128 * h:128 * h + 128] = acc
        yield
    for v in range(NV):
        phacc[v] += sums[v]
    r3 = lax.broadcasted_iota(jnp.int32, (256, 128), 0)
    c3 = lax.broadcasted_iota(jnp.int32, (256, 128), 1)
    fold = jnp.where(c3 == (r3 // 128) * 64 + 4 * t + (r3 % 128) // PITCH, 1.0, 0.0).astype(f32)
    acc_ref[...] += jnp.dot(aes[...], fold, preferred_element_type=f32, precision=lax.Precision.HIGHEST)


def pack_sums(phacc, acc_ref, el_ref):
    f32 = jnp.float32
    lane = lax.broadcasted_iota(jnp.int32, (1, 128), 1)
    sums = jnp.concatenate([jnp.sum(phacc[v], axis=0, keepdims=True) for v in range(NV)]
                           + [jnp.zeros((16 - NV, 128), f32)], axis=0)
    sums = jnp.sum(sums, axis=1, keepdims=True)
    phonon = jnp.where(lane == 96, sums[0:8], 0.0) + jnp.where(lane == 97, sums[8:16], 0.0)
    for b in range(16):
        out = phonon
        for u in range(3):
            a = NB * (b // 2) + 8 * u
            piece = jnp.where(lane // 64 == b % 2, acc_ref[a:a + 8, :], 0.0)
            shift = (32 * u + 64 * (b % 2)) % 128
            out = out + (pltpu.roll(piece, shift, 1) if shift else piece)
        el_ref[4 * (b % 4) + b // 4] = out


def run(*steps):
    steps = list(steps)
    while steps:
        for s in list(steps):
            if next(s, "end") == "end":
                steps.remove(s)


def rotate(coup_ref, rot_ref, sp, us, rs_ref):
    f32, bf16 = jnp.float32, jnp.bfloat16
    row = lax.broadcasted_iota(jnp.int32, (128, 1), 0)
    v = row % NM
    s = v % NV
    far = jnp.where(s >= 5, 1, 0)
    column = 256 * (v // NV) + 128 * far + NB * (s - 5 * far) + row // NM
    column = jnp.where(row < 3 * NM, column, -1024)
    lanes = lax.broadcasted_iota(jnp.int32, (128, 1024), 1)
    for g in range(8):
        sp[128 * g:128 * g + 128, :] = jnp.where(lanes == column + 3 * g, 1.0, 0.0).astype(bf16)
    rot = rot_ref[...].astype(f32)
    for q in range(4):
        rq = jnp.concatenate([rot[:, q, :], jnp.zeros((NM, 128 - NM), f32)], axis=1)
        rp = [(pltpu.roll(rq, NM * a, 1) if a else rq).astype(bf16) for a in range(3)]
        for r in range(2):
            ct = jnp.transpose(coup_ref[q, r].astype(f32))
            u = jnp.zeros((8 * NB, 128), f32)
            for a in range(3):
                rows = jnp.concatenate([ct[NB * (3 * g + a):NB * (3 * g + a) + NB] for g in range(8)], axis=0)
                u = u + jnp.dot(rows.astype(bf16), rp[a], preferred_element_type=f32)
            for g in range(8):
                us[NB * (2 * q + r):NB * (2 * q + r) + NB, 128 * g:128 * g + 128] = u[NB * g:NB * g + NB]
    out = jnp.dot(us[...].astype(bf16), sp[...], preferred_element_type=f32).astype(bf16)
    for q in range(4):
        for b in range(4):
            rs_ref[q, b] = out[48 * q:48 * q + 48, 256 * b:256 * b + 256]


def own_slice(z, ev_ref, en_ref, win_ref):
    f32, bf16 = jnp.float32, jnp.bfloat16
    lane = lax.broadcasted_iota(jnp.int32, (1, 128), 1)
    pick = lax.broadcasted_iota(jnp.int32, (32, 128), 0) == 4 * z + lane // PITCH
    lim = jnp.dot(jnp.broadcast_to(win_ref[...], (8, 32)).astype(bf16), jnp.where(pick, 1.0, 0.0).astype(bf16),
                  preferred_element_type=f32)[0:1]
    band = lane % PITCH
    wide = jnp.dot(ev_ref[...], jnp.where(pick, 1.0, 0.0).astype(bf16), preferred_element_type=f32)
    row = lax.broadcasted_iota(jnp.int32, (NB * NB, 128), 0)
    keep = (row % NB == band) & (band.astype(f32) < lim)
    r4 = lax.broadcasted_iota(jnp.int32, (NB, NB * NB), 0)
    c4 = lax.broadcasted_iota(jnp.int32, (NB, NB * NB), 1)
    gather = jnp.where(c4 // NB == r4, 1.0, 0.0).astype(bf16)
    vectors = jnp.dot(gather, jnp.where(keep, wide, 0.0).astype(bf16), preferred_element_type=f32)
    levels = jnp.dot(en_ref[...], jnp.where(pick, 1.0, 0.0).astype(f32), preferred_element_type=f32,
                     precision=lax.Precision.HIGHEST)
    levels = jnp.where(lax.broadcasted_iota(jnp.int32, (NB, 128), 0) == band, levels, 0.0)
    return vectors.astype(bf16), jnp.sum(levels, axis=0, keepdims=True)


def place():
    ka, pb, row = lax.axis_index("ka"), lax.axis_index("pb"), lax.axis_index("row")
    return ka // 2, ka % 2, row, pb // 8, pb % 8


def device(y, core, x, y_lo, z):
    return {"ka": 2 * y + core, "pb": 8 * y_lo + z, "row": x}


def phases(c, kp_ref, lat_ref, widen, pscr):
    f32 = jnp.float32
    lat = jnp.transpose(jnp.concatenate([lat_ref[...].astype(f32), jnp.zeros((5, NR), f32)], axis=0))
    for u in range(4):
        cols = pl.ds(pl.multiple_of(256 * u + 128 * c, 128), 128)
        arg = (lat[:, 0:1] * kp_ref[0:1, cols] + lat[:, 1:2] * kp_ref[1:2, cols]
               + lat[:, 2:3] * kp_ref[2:3, cols])
        ph = jnp.cos(2.0 * math.pi * arg).astype(jnp.bfloat16)
        pscr[128 * u:128 * u + 128, :] = lax.dot_general(
            ph, widen, (((0,), (0,)), ((), ())), preferred_element_type=f32)


def mega_kernel(kq_ref, freq_ref, kp_ref, lat_ref, coup_ref, rot_ref, ev_ref, en_ref, win_ref,
                electron_ref, phonon_ref, sp, us, rs_ref, rt, eig, etab, pscr, etscr, wa, wb, xa, xb, bds, ybufs, aes, phacc, acc_ref,
                el, got, tiles2, got2, mine, peers, half,
                own, r_send, r_recv, t_send, t_recv, e_send, e_recv,
                up_send, up_recv, dn_send, dn_recv, ut_send, ut_recv, dt_send, dt_recv,
                rf_send, rf_recv, ef_send, ef_recv, tf_send, tf_recv,
                a_send, a_recv, b_send, b_recv, p_send, p_recv):
    f32 = jnp.float32
    y, c, x, w, z = place()
    me = y * 4 + x
    partner = device(y, 1 - c, x, w, z)
    above = device(y, c, x, w, (z + 1) % 8)
    below = device(y, c, x, w, (z + 7) % 8)
    plane, column = [], []
    for d in range(1, 16):
        yy, xx = (y + d // 4) % 4, (x + d % 4) % 4
        plane.append((yy, xx, device(yy, c, xx, w, z)))
        ww, zz = (w + d // 8) % 2, (z + d % 8) % 8
        column.append(device(y, c, x, ww, zz))

    barrier = pltpu.get_barrier_semaphore()
    for target in [o[2] for o in plane] + column + [partner]:
        pl.semaphore_signal(barrier, inc=1, device_id=target, device_id_type=pl.DeviceIdType.MESH)

    here = 32 * z + 16 * c + me
    eig[here], etab[pl.ds(here, 1), :] = own_slice(z, ev_ref, en_ref, win_ref)
    rotate(coup_ref, rot_ref, sp, us, rs_ref)
    pl.semaphore_wait(barrier, 31)

    copies = []

    def send(src, dst, s, r, target):
        cp = pltpu.make_async_remote_copy(src_ref=src, dst_ref=dst, send_sem=s, recv_sem=r, device_id=target,
                                          device_id_type=pl.DeviceIdType.MESH)
        cp.start()
        return cp

    def arrival(ref, recv):
        pltpu.make_async_copy(ref, ref, recv).wait()

    def tiles(t, core):
        return eig.at[pl.ds(32 * t + 16 * core, 16)]

    def rows(t, core):
        return etab.at[pl.ds(pl.multiple_of(32 * t + 16 * core, 16), 16)]

    for n, (yy, xx, target) in enumerate(plane):
        copies.append(send(eig.at[here], eig.at[here], e_send.at[n], e_recv.at[n], target))
        copies.append(send(etab.at[pl.ds(here, 1)], etab.at[pl.ds(here, 1)], t_send.at[n], t_recv.at[n], target))
    for n, (yy, xx, target) in enumerate(plane):
        copies.append(send(rs_ref.at[yy, xx], rt.at[y, c, x], r_send.at[n], r_recv.at[n], target))

    local = pltpu.make_async_copy(rs_ref.at[y, x], rt.at[y, c, x], own.at[0])
    local.start()
    spread, widen = constants()
    phases(c, kp_ref, lat_ref, widen, pscr)
    bds[...] = jnp.zeros_like(bds)
    phacc[...] = jnp.zeros_like(phacc)
    acc_ref[...] = jnp.zeros_like(acc_ref)

    def ring(step):
        up, dn = (z + 8 - step) % 8, (z + step) % 8
        if step:
            arrival(tiles(up, c), up_recv.at[step - 1])
            arrival(rows(up, c), ut_recv.at[step - 1])
        if step < 4:
            send(tiles(up, c), tiles(up, c), up_send.at[step], up_recv.at[step], above)
            send(rows(up, c), rows(up, c), ut_send.at[step], ut_recv.at[step], above)
        if 0 < step < 4:
            arrival(tiles(dn, c), dn_recv.at[step - 1])
            arrival(rows(dn, c), dt_recv.at[step - 1])
        if step < 3:
            send(tiles(dn, c), tiles(dn, c), dn_send.at[step], dn_recv.at[step], below)
            send(rows(dn, c), rows(dn, c), dt_send.at[step], dt_recv.at[step], below)
        for f, t in [(step, up)] + ([(4 + step, dn)] if 0 < step < 4 else []):
            send(tiles(t, c), tiles(t, c), ef_send.at[f], ef_recv.at[f], partner)
            send(rows(t, c), rows(t, c), tf_send.at[f], tf_recv.at[f], partner)

    def slice_of(f):
        return (z + 8 - f) % 8 if f < 5 else (z + f - 4) % 8

    local.wait()
    for n in range(15):
        d = n + 1
        b = (y + 4 - d // 4) % 4 * 4 + (x + 4 - d % 4) % 4
        arrival(eig.at[32 * z + 16 * c + b], e_recv.at[n])
        arrival(etab.at[pl.ds(32 * z + 16 * c + b, 1)], t_recv.at[n])
    ring(0)
    ring(1)
    for dy in range(4):
        yy = (y + 4 - dy) % 4
        for dx in range(4):
            if dy or dx:
                arrival(rt.at[yy, c, (x + 4 - dx) % 4], r_recv.at[4 * dy + dx - 1])
        copies.append(send(rt.at[yy, c], rt.at[yy, c], rf_send.at[dy], rf_recv.at[dy], partner))
    for dy in range(4):
        arrival(rt.at[(y + 4 - dy) % 4, 1 - c], rf_recv.at[dy])

    def slice_at(i):
        return (z + 8 + (1 - 2 * (i % 2)) * ((i + 1) // 2)) % 8

    rargs = (c, rt, eig, spread, pscr, etscr, (wa, wb))
    fargs = (c, y, x, kq_ref, freq_ref, eig, etab)
    sums = (bds, ybufs, aes, phacc, acc_ref)

    def first(i, _):
        for step in (2, 3, 4):
            pl.when(i == step - 2 + 2 * (step // 4))(lambda step=step: ring(step))
        run(right_steps(i, slice_at(i), *rargs, xa))
        return 0
    lax.fori_loop(0, 5, first, 0)

    for f in range(8):
        arrival(tiles(slice_of(f), 1 - c), ef_recv.at[f])
        arrival(rows(slice_of(f), 1 - c), tf_recv.at[f])

    def both_stages(i, _):
        run(final_steps(i, slice_at(i), *fargs, xa, *sums), right_steps(i, slice_at(i + 5), *rargs, xb))
        return 0
    lax.fori_loop(0, 3, both_stages, 0)

    def late(i, _):
        run(final_steps(i, slice_at(i), *fargs, xa, *sums))
        return 0
    lax.fori_loop(3, 5, late, 0)

    def last(i, _):
        run(final_steps(i, slice_at(i + 5), *fargs, xb, *sums))
        return 0
    lax.fori_loop(0, 3, last, 0)
    pack_sums(phacc, acc_ref, el)

    for d in range(1, 4):
        xx = (x + d) % 4
        copies.append(send(el.at[pl.ds(4 * xx, 4)], got.at[pl.ds(4 * x, 4)], a_send.at[d - 1], a_recv.at[d - 1],
                           device(y, c, xx, w, z)))
    for d in range(1, 4):
        arrival(got.at[pl.ds(4 * ((x + 4 - d) % 4), 4)], a_recv.at[d - 1])
    lane = lax.broadcasted_iota(jnp.int32, (8, 128), 1)
    for yy in range(4):
        total = jnp.zeros((8, 128), f32)
        for s in range(4):
            tile = jnp.where(x == s, el[4 * s + yy], got[4 * s + yy])
            total = total + jnp.where(lane < 96, tile, 0.0)
            phonon = jnp.where((lane == 96) | (lane == 97), tile, 0.0)
            total = total + (pltpu.roll(phonon, 2 * s, 1) if s else phonon)
        tiles2[yy] = total
    for d in range(1, 4):
        yy = (y + d) % 4
        copies.append(send(tiles2.at[yy], got2.at[y], a_send.at[d + 2], a_recv.at[d + 2], device(yy, c, x, w, z)))
    for d in range(1, 4):
        arrival(got2.at[(y + 4 - d) % 4], a_recv.at[d + 2])
    total = jnp.zeros((8, 128), f32)
    phonon = jnp.zeros((8, 128), f32)
    for s in range(4):
        tile = jnp.where(y == s, tiles2[s], got2[s])
        total = total + jnp.where(lane < 96, tile, 0.0)
        phonon = phonon + pltpu.roll(jnp.where((lane >= 96) & (lane < 104), tile, 0.0), 32 + 8 * s, 1)
    mine[...] = total
    half[0] = phonon
    for n, target in enumerate(column):
        copies.append(send(mine, peers.at[w * 8 + z], b_send.at[n], b_recv.at[n], target))
    copies.append(send(half.at[0], half.at[1], p_send.at[0], p_recv.at[0], partner))
    arrival(half.at[1], p_recv.at[0])
    both = half[0] + half[1]
    owner = lax.broadcasted_iota(jnp.int32, (8, 128), 0)
    spot = lax.broadcasted_iota(jnp.int32, (128, 128), 0)
    mode = lax.broadcasted_iota(jnp.int32, (128, 128), 1)
    result = jnp.zeros((8, 128), f32)
    for s in range(8 if NV > 8 else NV):
        line = jnp.where(lane // 8 == owner, both[s:s + 1], 0.0)
        inner = 8 * (spot % 2) + s
        to = jnp.where((inner < NV) & (mode == NV * (spot // 2 % 4) + inner), 1.0, 0.0).astype(f32)
        result = result + jnp.dot(line, to, preferred_element_type=f32, precision=lax.Precision.HIGHEST)
    phonon_ref[...] = result[0:4, 0:NM]
    for n in range(15):
        d = n + 1
        arrival(peers.at[(w + 2 - d // 8) % 2 * 8 + (z + 8 - d % 8) % 8], b_recv.at[n])
    acc = jnp.zeros((8, 128), f32)
    for s in range(16):
        acc = acc + jnp.where(w * 8 + z == s, total, peers[s])
    acc = jnp.concatenate([acc, pltpu.roll(acc, 96, 1), pltpu.roll(acc, 64, 1)], axis=0)
    electron_ref[...] = acc[:, 0:32]

    for cp in copies:
        cp.wait_send()
    for step in range(4):
        arrival(tiles(z, c), up_send.at[step])
        arrival(rows(z, c), ut_send.at[step])
        if step < 3:
            arrival(tiles(z, c), dn_send.at[step])
            arrival(rows(z, c), dt_send.at[step])
    for f in range(8):
        arrival(tiles(z, c), ef_send.at[f])
        arrival(rows(z, c), tf_send.at[f])


def mega(kq, freq, kp, lat, coup, rot, ev, en, win):
    f32, bf16 = jnp.float32, jnp.bfloat16
    smem = pl.BlockSpec(memory_space=pltpu.SMEM)
    vmem = pl.BlockSpec(memory_space=pltpu.VMEM)
    dma = pltpu.SemaphoreType.DMA
    return pl.pallas_call(
        mega_kernel,
        out_shape=(jax.ShapeDtypeStruct((NB, 32), f32), jax.ShapeDtypeStruct((4, NM), f32)),
        in_specs=[smem, smem] + [vmem] * 7,
        out_specs=(vmem, vmem),
        scratch_shapes=[
            pltpu.VMEM((1024, 1024), bf16), pltpu.VMEM((192, 1024), f32), pltpu.VMEM((4, 4, 48, 256), bf16),
            pltpu.VMEM((4, 2, 4, 48, 256), bf16), pltpu.VMEM((256, NB, 128), bf16), pltpu.VMEM((256, 128), f32),
            pltpu.VMEM((512, NR * NB), f32), pltpu.VMEM((2048, 384), f32),
            pltpu.VMEM((384, NR * NB), bf16), pltpu.VMEM((384, NR * NB), bf16), pltpu.VMEM((5, 1536, 256), f32), pltpu.VMEM((3, 1536, 256), f32),
            pltpu.VMEM((4, 256, 256), bf16), pltpu.VMEM((4, NV * NB, 256), f32), pltpu.VMEM((8 * NB, 256), f32),
            pltpu.VMEM((NV, 8, 128), f32), pltpu.VMEM((8 * NB, 128), f32),
            pltpu.VMEM((16, 8, 128), f32), pltpu.VMEM((16, 8, 128), f32), pltpu.VMEM((4, 8, 128), f32),
            pltpu.VMEM((4, 8, 128), f32), pltpu.VMEM((8, 128), f32),
            pltpu.VMEM((16, 8, 128), f32), pltpu.VMEM((2, 8, 128), f32),
            dma((1,)), dma((15,)), dma((15,)), dma((15,)), dma((15,)), dma((15,)), dma((15,)),
            dma((4,)), dma((4,)), dma((3,)), dma((3,)), dma((4,)), dma((4,)), dma((3,)), dma((3,)),
            dma((4,)), dma((4,)), dma((8,)), dma((8,)), dma((8,)), dma((8,)),
            dma((6,)), dma((6,)), dma((15,)), dma((15,)), dma((1,)), dma((1,))],
        compiler_params=pltpu.CompilerParams(collective_id=0, has_side_effects=True, vmem_limit_bytes=60 << 20),
        name="linewidths",
    )(kq, freq, kp, lat, coup, rot, ev, en, win)


def on_device(coupling, rotation, freq, eigvec, energies, window, kq_index, kpoints, lattice):
    electron, phonon = mega(kq_index, freq, kpoints.T, lattice.T, coupling.reshape(4, 2, NM, NB * NB),
                            rotation.transpose(1, 0, 2), eigvec.transpose(1, 2, 0).reshape(NB * NB, 32), energies.T,
                            window.reshape(1, 32))
    norm = 1.0 / (math.sqrt(2.0 * math.pi) * SIGMA)
    return electron.T * (norm / 55296.0), phonon * (norm / 24576.0)


def solution(mesh):
    return jax.shard_map(
        on_device,
        mesh=mesh,
        in_specs=(
            P("pb", ("ka", "row"), None),
            P("pb", None, None),
            P("pb", None),
            P(("ka", "row"), None, None),
            P(("ka", "row"), None),
            P(("ka", "row")),
            P("pb", None),
            P(),
            P(),
        ),
        out_specs=(P(("ka", "row"), None), P("pb", None)),
        check_vma=False,
    )
```
